32 devices in a mesh: groups: 2 (over y), tm: 4 (over z), space: 2 (over x), chan: 2 (over core).
Axes of the slice: x: 2, y: 2, z: 4, core: 2. Of those that a mesh axis runs over, the one named last changes fastest.
Arguments:
- frames: bfloat16 [32, 64, 64, 256], P(('groups', 'tm'), 'chan', 'space'), parts along dimension 0, may hold values from -6 to 6
- conv_taps: float32 [64, 9], P('chan'), may hold values from -2 to 2
- pooling: float32 [64, 256], P('space'), may hold values from -0.0625 to 0.0625
- gain_matrix: float32 [256, 128], P(None, ('space', 'chan')), may hold values from -0.5 to 0.5
- transition: float32 [256, 256], replicated, as said below
- update_map: float32 [256, 256], replicated, as said below
- quiet_root: float32 [256, 256], replicated, as said below
- observed_root: float32 [256, 256], replicated, as said below
- init_mean: float32 [512], P('groups'), parts along dimension 0, may hold values from -6 to 6
- init_root: float32 [512, 256], P('groups'), parts along dimension 0, as said below
- observed: int32 [32], P(('groups', 'tm')), parts along dimension 0, may hold values 0 or 1
Outputs:
- filtered_means: float32 [32, 256], P(('groups', 'tm')), parts along dimension 0
- block_roots: float32 [8, 256, 256], P(('groups', 'tm')), parts along dimension 0
- tap_gradient: float32 [8, 64, 9], P(('groups', 'tm'), 'chan'), parts along dimension 0
The draws below stay inside these ranges and needn't reach their ends.
There are 2 independent parts, one for each index of `groups`. The reference program is written for one: setup_inputs(seed, part) draws one part's arguments, and reference() takes and returns one part's arrays. A program takes and returns all parts, laid end to end along the dimension named above; an argument that names none is the same for every part. Nothing has to cross between parts.
Inputs may be any that keep to these rules, and one draw needn't show every extreme that they name: transition and update_map are upper triangular, with the same diagonal entries where these exceed 0.8. transition is upper triangular. `quiet_root`: upper triangular with a positive diagonal. `observed_root`: upper triangular with a positive diagonal. `init_root`: upper triangular with a positive diagonal.
All inputs are finite; a program needn't handle non-finite values. No bound on the sum of `observed` on one device may be relied on, other than what follows from the above.
Results may differ from the reference program's by a relative error of at most 0.0003.
Values may be sent and summed in bfloat16 or wider, within the bound.
No kernel may reach another device: no remote copies, remote signals or barrier semaphores. Data moves between devices by JAX's collectives and lax.ppermute only.
A program may use at most 64 MiB of HBM per device.

```python
import math
import jax
import jax.numpy as jnp
from jax import lax

S = 256
CH = 64
W = 256
DILATION_STEP = 2
TB = 4
ROWS_DEV = 32
NT = 16
H = 64
OBS = 128
N_TM = 4
N_SPACE = 2


def channel_rates(key):
    pick_key = jax.random.fold_in(key, 101)
    level_key = jax.random.fold_in(key, 102)
    fast_key = jax.random.fold_in(key, 103)
    slow_share = 0.5
    is_slow = jax.random.uniform(pick_key, (S,), jnp.float32) < slow_share
    slow_rates = 0.1 ** (jax.random.uniform(level_key, (S,), jnp.float32, 0.2, 0.5) / NT)
    fast_rates = jax.random.uniform(fast_key, (S,), jnp.float32, 0.3, 0.7)
    return jnp.where(is_slow, slow_rates, fast_rates)


def coupled(key, rates, spread):
    entries = jax.random.normal(key, (S, S), jnp.float32) * (spread / math.sqrt(S))
    damping = 1.0 - rates[:, None] * rates[None, :]
    return jnp.diag(rates) + jnp.triu(entries * damping, 1)


def triangular_root(key):
    diag_key = jax.random.fold_in(key, 301)
    off_key = jax.random.fold_in(key, 302)
    upper_end = 0.6
    levels = jax.random.uniform(diag_key, (S,), jnp.float32, math.log(0.3), math.log(upper_end))
    entries = jax.random.normal(off_key, (S, S), jnp.float32) * (0.15 / math.sqrt(S))
    return jnp.diag(jnp.exp(levels)) + jnp.triu(entries, 1)


def draw_transition(key, part):
    rates = channel_rates(key)
    return coupled(jax.random.fold_in(key, 201), rates, 0.4)


def draw_update_map(key, part):
    rates = channel_rates(key)
    shrink = jax.random.uniform(jax.random.fold_in(key, 202), (S,), jnp.float32, 0.5, 1.0)
    shrunk = jnp.where(rates > 0.8, rates, rates * shrink)
    return coupled(jax.random.fold_in(key, 203), shrunk, 0.4)


def draw_quiet_root(key, part):
    return triangular_root(jax.random.fold_in(key, 1))


def draw_observed_root(key, part):
    return triangular_root(jax.random.fold_in(key, 2))


def draw_init_root(key, part):
    return triangular_root(jax.random.fold_in(key, 3))


def touch_ends(values, key, smallest, top_value):
    place = [jax.random.randint(jax.random.fold_in(key, axis), (), 0, length) for axis, length in enumerate(values.shape)]
    main_axis = values.shape.index(max(values.shape))
    next_to = place[:main_axis] + [(place[main_axis] + 1) % values.shape[main_axis]] + place[main_axis + 1:]
    return values.at[tuple(place)].set(smallest).at[tuple(next_to)].set(top_value)


def block_levels(stream_key, dims, pieces, low, largest):
    def one(dim, shards_of):
        steps = jax.random.uniform(jax.random.fold_in(jax.random.fold_in(stream_key, 6), dim), (shards_of,), jnp.float32, low / len(pieces), largest / len(pieces))
        return jnp.repeat(jnp.exp(steps), dims[dim] // shards_of).reshape((-1,) + (1,) * (len(dims) - dim - 1))

    level = one(*pieces[0])
    for cut in pieces[1:]:
        level = level * one(*cut)
    return level


def centred(rng, extent, deviation, limit, cuts=(), kind=jnp.bfloat16):
    result = deviation * jax.random.normal(rng, extent, jnp.float32)
    if cuts:
        result = result * block_levels(rng, extent, cuts, -0.22, 0.18)
    return jnp.clip(result, -limit, limit).astype(kind)


def setup_inputs(seed: int = 0, part: int = 0) -> dict:
    splits = jax.random.split(jax.random.key(seed), 12)
    own_keys = jax.random.split(jax.random.fold_in(splits[11], part), 12)
    frames = centred(own_keys[0], (NT, CH, H, W), 1.0, 6.0, ((0, 4), (1, 2), (2, 2)))
    conv_taps = centred(splits[1], (CH, 9), 0.33, 2.0, ((0, 2),), jnp.float32)
    pooling = centred(splits[2], (H, W), (ROWS_DEV * W) ** -0.5, 0.0625, ((0, 2),), jnp.float32)
    gain_matrix = centred(splits[3], (S, OBS), OBS ** -0.5, 0.5, ((1, 4),), jnp.float32)
    transition = draw_transition(jax.random.fold_in(splits[11], 71), part)
    update_map = draw_update_map(jax.random.fold_in(splits[11], 71), part)
    quiet_root = draw_quiet_root(jax.random.fold_in(splits[11], 71), part)
    observed_root = draw_observed_root(jax.random.fold_in(splits[11], 71), part)
    init_mean = centred(own_keys[8], (S,), 1.0, 6.0, (), jnp.float32)
    init_root = draw_init_root(jax.random.fold_in(jax.random.fold_in(splits[11], part), 71), part)
    observed = touch_ends((jax.random.randint(own_keys[10], (NT,), 0, 2) < 1).astype(jnp.int32), jax.random.fold_in(own_keys[10], 1), 0, 1)
    return {"frames": frames, "conv_taps": conv_taps, "pooling": pooling, "gain_matrix": gain_matrix, "transition": transition, "update_map": update_map, "quiet_root": quiet_root, "observed_root": observed_root, "init_mean": init_mean, "init_root": init_root, "observed": observed}


precise = lax.Precision.HIGHEST

def upper_factor(gram_sum):
    is_blank = jnp.trace(gram_sum) == 0.0
    unit_matrix = jnp.eye(gram_sum.shape[0], dtype=jnp.float32)
    safe_gram = jnp.where(is_blank, unit_matrix, gram_sum)
    return jnp.where(is_blank, jnp.float32(0.0), jnp.linalg.cholesky(safe_gram).T)

def response_of(frame_advance, conv_taps):
    frame_height = frame_advance.shape[1]
    column_list = frame_advance.shape[2]
    padded_frame = jnp.pad(frame_advance.astype(jnp.float32), ((0, 0), (DILATION_STEP, DILATION_STEP), (DILATION_STEP, DILATION_STEP)))
    window_views = [padded_frame[:, left_element * DILATION_STEP:left_element * DILATION_STEP + frame_height, right_element * DILATION_STEP:right_element * DILATION_STEP + column_list] for left_element in range(3) for right_element in range(3)]
    response = jnp.zeros(frame_advance.shape, jnp.float32)
    for k in range(9):
        response = response + conv_taps[:, k][:, None, None] * window_views[k]
    return (response, window_views)

def reference(frames, conv_taps, pooling, gain_matrix, transition, update_map, quiet_root, observed_root, init_mean, init_root, observed):
    frame_height = frames.shape[2]
    column_list = frames.shape[3]
    pool_tiles = pooling.reshape(N_SPACE, ROWS_DEV, column_list)

    def per_step(inputs):
        frame_advance, flag = inputs
        response, window_views = response_of(frame_advance, conv_taps)
        tiles = response.reshape(CH, N_SPACE, ROWS_DEV, column_list)
        tile_sums = jnp.einsum('cshw,shw->sc', tiles, pool_tiles, precision=precise).reshape(N_SPACE * CH)
        weight = flag.astype(jnp.float32) / (frame_height * column_list)
        grad_step = jnp.stack([jnp.sum(response * window_views[k], axis=(1, 2)) for k in range(9)], axis=1) * weight
        return (tile_sums, grad_step)
    tile_sums, grad_steps = lax.map(per_step, (frames, observed))
    weights = observed.astype(jnp.float32)
    shifts = jnp.dot(tile_sums.astype(jnp.float32), gain_matrix.T.astype(jnp.float32), precision=precise, preferred_element_type=jnp.float32) * weights[:, None]
    tap_gradient = jnp.sum(grad_steps.reshape(N_TM, TB, CH, 9), axis=1)

    def advance(state, inputs):
        mean_now, root_now = state
        flag, shift_now = inputs
        step_map = jnp.where(flag > 0, update_map, transition)
        step_root = jnp.where(flag > 0, observed_root, quiet_root)
        mean_next = jnp.dot(step_map.astype(jnp.float32), mean_now.astype(jnp.float32), precision=precise, preferred_element_type=jnp.float32) + shift_now
        carried = jnp.dot(root_now.astype(jnp.float32), step_map.T.astype(jnp.float32), precision=precise, preferred_element_type=jnp.float32)
        gram_sum = jnp.dot(carried.T.astype(jnp.float32), carried.astype(jnp.float32), precision=precise, preferred_element_type=jnp.float32)
        gram_sum = gram_sum + jnp.dot(step_root.T.astype(jnp.float32), step_root.astype(jnp.float32), precision=precise, preferred_element_type=jnp.float32)
        root_next = upper_factor(gram_sum)
        return ((mean_next, root_next), (mean_next, root_next))
    final_state, outputs = lax.scan(advance, (init_mean, init_root), (observed, shifts))
    filtered_means, all_roots = outputs
    block_roots = all_roots[TB - 1::TB]
    return (filtered_means, block_roots, tap_gradient)
```

```python
import jax
import jax.numpy as jnp
from jax import lax
from jax.experimental import pallas as pl
from jax.experimental.pallas import tpu as pltpu
from jax.sharding import PartitionSpec as P

DILATION_STEP = 2
PANEL = 32
GROUP = 8
LANES = 128
F32 = jnp.float32
BF16 = jnp.bfloat16

precise = lax.Precision.HIGHEST


def extended(block, axis, dim, width):
    count = lax.axis_size(axis)
    forward = [(i, i + 1) for i in range(count - 1)]
    backward = [(target, source) for source, target in forward]
    low = lax.ppermute(
        lax.slice_in_dim(block, block.shape[dim] - width, None, axis=dim), axis, forward
    )
    high = lax.ppermute(lax.slice_in_dim(block, 0, width, axis=dim), axis, backward)
    return jnp.concatenate([low, block, high], axis=dim)


def history(own, axis):
    count = lax.axis_size(axis)
    held = own
    reach = 1
    while reach < count:
        pairs = [(i, i + reach) for i in range(count - reach)]
        held = jnp.concatenate([held, lax.ppermute(held, axis, pairs)], axis=0)
        reach *= 2
    return held


def split(x):
    high = x.astype(BF16)
    return high, (x - high.astype(F32)).astype(BF16)


def contract(a, b, dims):
    return lax.dot_general(a, b, (dims, ((), ())), preferred_element_type=F32)


def three_pass(a, b, dims):
    return (
        contract(a[0], b[0], dims)
        + contract(a[0], b[1], dims)
        + contract(a[1], b[0], dims)
    )


NN = ((1,), (0,))
NT = ((1,), (1,))
TN = ((0,), (0,))


def prepare_kernel(
    transition, update_map, quiet_root, observed_root, init_root,
    map_high, map_low, grams, first_gram,
):
    for which, ref in ((0, transition), (1, update_map)):
        high, low = split(ref[...])
        map_high[which] = high
        map_low[which] = low
    for which, ref in ((0, quiet_root), (1, observed_root)):
        pair = split(ref[...])
        grams[which] = three_pass(pair, pair, TN)
    pair = split(init_root[...])
    first_gram[...] = three_pass(pair, pair, TN)


def prepare(transition, update_map, quiet_root, observed_root, init_root):
    size = transition.shape[0]
    return pl.pallas_call(
        prepare_kernel,
        out_shape=(
            jax.ShapeDtypeStruct((2, size, size), BF16),
            jax.ShapeDtypeStruct((2, size, size), BF16),
            jax.ShapeDtypeStruct((2, size, size), F32),
            jax.ShapeDtypeStruct((size, size), F32),
        ),
        name="prepare",
    )(transition, update_map, quiet_root, observed_root, init_root)


def upper_factor(gram, out, high, low):
    size = gram.shape[0]
    halves = size // LANES
    tile = (GROUP, LANES)
    zero = jnp.zeros(tile, F32)
    sub = lax.broadcasted_iota(jnp.int32, tile, 0)
    lane = lax.broadcasted_iota(jnp.int32, tile, 1)
    count = PANEL // GROUP
    for top in range(0, size, PANEL):
        first = top // LANES
        start = first * LANES
        panel = gram[top : top + PANEL, start:]
        if top:
            left = (high[:top, top : top + PANEL], low[:top, top : top + PANEL])
            panel = panel - three_pass(left, (high[:top, start:], low[:top, start:]), TN)
        places = range(halves - first)
        part = [
            [
                panel[GROUP * i : GROUP * (i + 1), LANES * h : LANES * (h + 1)]
                for h in places
            ]
            for i in range(count)
        ]
        done = [[zero for _ in places] for _ in range(count)]
        for g in range(count):
            base = top + GROUP * g
            here, at = base // LANES - first, base % LANES
            live = range(here, halves - first)
            column = {
                i: [
                    jnp.broadcast_to(part[i][here][:, at + j : at + j + 1], tile)
                    for j in range(GROUP)
                ]
                for i in range(g, count)
            }
            pivot = {
                (j, m): jnp.broadcast_to(column[g][m][j : j + 1, :], tile)
                for j in range(GROUP)
                for m in range(j, GROUP)
            }
            factor, scale = {}, []
            for j in range(GROUP):
                scale.append(lax.rsqrt(pivot[j, j]))
                for m in range(j + 1, GROUP):
                    factor[j, m] = pivot[j, m] * scale[j]
                for i in range(j + 1, GROUP):
                    for m in range(i, GROUP):
                        pivot[i, m] = pivot[i, m] - factor[j, i] * factor[j, m]
            rows = {}
            for h in live:
                rows[h] = []
                for j in range(GROUP):
                    value = jnp.broadcast_to(part[g][h][j : j + 1, :], tile)
                    for i in range(j):
                        value = value - factor[i, j] * rows[h][i]
                    rows[h].append(value * scale[j])
                value = rows[h][0]
                for j in range(1, GROUP):
                    value = jnp.where(sub == j, rows[h][j], value)
                if h == here:
                    value = jnp.where(lane - at >= sub, value, 0.0)
                done[g][h] = value
            for i in range(g + 1, count):
                left = []
                for j in range(GROUP):
                    value = column[i][j]
                    for m in range(j):
                        value = value - factor[m, j] * left[m]
                    left.append(value * scale[j])
                for h in live:
                    value = part[i][h]
                    for j in range(GROUP):
                        value = value - left[j] * rows[h][j]
                    part[i][h] = value
        for i in range(count):
            low_row = top + GROUP * i
            for h in range(halves):
                value = done[i][h - first] if h >= first else zero
                out[low_row : low_row + GROUP, LANES * h : LANES * (h + 1)] = value
        if top + PANEL < size:
            rows_high, rows_low = split(out[top : top + PANEL, :])
            high[top : top + PANEL, :] = rows_high
            low[top : top + PANEL, :] = rows_low


def covariance_kernel(steps, place, flags, map_high, map_low, grams, first_gram, out, gram, high, low):
    index = place[0]
    gram[...] = first_gram[...]

    def step(t, carry):
        flag = flags[(index - t // steps) * steps + t % steps]
        map_pair = (map_high[flag], map_low[flag])
        carried = three_pass(map_pair, split(gram[...]), NN)
        gram[...] = three_pass(split(carried), map_pair, NT) + grams[flag]
        return carry

    lax.fori_loop(0, (index + 1) * steps, step, 0)
    upper_factor(gram, out, high, low)


def covariance(place, flags, steps, map_high, map_low, grams, first_gram):
    size = first_gram.shape[0]
    vmem = pl.BlockSpec(memory_space=pltpu.VMEM)
    smem = pl.BlockSpec(memory_space=pltpu.SMEM)

    def kernel(*refs):
        covariance_kernel(steps, *refs)

    return pl.pallas_call(
        kernel,
        out_shape=jax.ShapeDtypeStruct((size, size), F32),
        in_specs=[smem, smem, vmem, vmem, vmem, vmem],
        out_specs=vmem,
        scratch_shapes=[
            pltpu.VMEM((size, size), F32),
            pltpu.VMEM((size, size), BF16),
            pltpu.VMEM((size, size), BF16),
        ],
        name="covariance",
    )(place, flags, map_high, map_low, grams, first_gram)


def means_kernel(steps, place, flags, map_high, map_low, shifts, init_mean, out):
    index = place[0]
    size = init_mean.shape[1]

    def step(t, mean):
        at = (index - t // steps) * steps + t % steps
        flag = flags[at]
        mean = three_pass(split(mean), (map_high[flag], map_low[flag]), NT)
        mean = mean + jnp.broadcast_to(shifts[pl.ds(at, 1), :], mean.shape)

        @pl.when(t // steps == index)
        def _():
            out[pl.ds(t % steps, 1), :] = mean[0:1]

        return mean

    lax.fori_loop(
        0, (index + 1) * steps, step, jnp.broadcast_to(init_mean[...], (GROUP, size))
    )


def means(place, flags, steps, map_high, map_low, shifts, init_mean):
    size = init_mean.shape[0]
    vmem = pl.BlockSpec(memory_space=pltpu.VMEM)
    smem = pl.BlockSpec(memory_space=pltpu.SMEM)

    def kernel(*refs):
        means_kernel(steps, *refs)

    return pl.pallas_call(
        kernel,
        out_shape=jax.ShapeDtypeStruct((steps, size), F32),
        in_specs=[smem, smem, vmem, vmem, vmem, vmem],
        out_specs=vmem,
        name="means",
    )(place, flags, map_high, map_low, shifts, init_mean[None])


def local(
    frames,
    conv_taps,
    pooling,
    gain_matrix,
    transition,
    update_map,
    quiet_root,
    observed_root,
    init_mean,
    init_root,
    observed,
):
    step_count, channels, row_tiles, column_list = frames.shape
    place = lax.axis_index("tm").astype(jnp.int32)[None]
    flags = history(observed, "tm")
    extended_frame = extended(frames, "space", 2, DILATION_STEP)
    map_high, map_low, grams, first_gram = prepare(
        transition, update_map, quiet_root, observed_root, init_root
    )
    extended_frame = jnp.pad(
        extended_frame, ((0, 0), (0, 0), (0, 0), (DILATION_STEP, DILATION_STEP))
    ).astype(jnp.float32)
    window_views = [
        extended_frame[
            :,
            :,
            left_element * DILATION_STEP : left_element * DILATION_STEP + row_tiles,
            right_element * DILATION_STEP : right_element * DILATION_STEP + column_list,
        ]
        for left_element in range(3)
        for right_element in range(3)
    ]
    response = jnp.zeros(frames.shape, jnp.float32)
    for k in range(9):
        response = response + conv_taps[:, k][None, :, None, None] * window_views[k]
    weights = observed.astype(jnp.float32)
    tile_sums = jnp.einsum("tchw,hw->tc", response, pooling, precision=precise)
    gain_part = (
        jnp.dot(tile_sums, gain_matrix.T, precision=precise, preferred_element_type=jnp.float32)
        * weights[:, None]
    )
    shifts = lax.psum(gain_part, ("space", "chan"))
    scaling = weights / (row_tiles * lax.axis_size("space") * column_list)
    grad_local = jnp.stack(
        [
            jnp.sum(response * window_views[k] * scaling[:, None, None, None], axis=(0, 2, 3))
            for k in range(9)
        ],
        axis=1,
    )
    tap_gradient = lax.psum(grad_local, "space")[None]
    all_shifts = history(shifts, "tm")
    root = covariance(place, flags, step_count, map_high, map_low, grams, first_gram)
    filtered_means = means(place, flags, step_count, map_high, map_low, all_shifts, init_mean)
    return (filtered_means, root[None], tap_gradient)


def solution(mesh):
    return jax.shard_map(
        local,
        mesh=mesh,
        in_specs=(
            P(("groups", "tm"), "chan", "space", None),
            P("chan", None),
            P("space", None),
            P(None, ("space", "chan")),
            P(),
            P(),
            P(),
            P(),
            P("groups"),
            P("groups", None),
            P(("groups", "tm")),
        ),
        out_specs=(
            P(("groups", "tm"), None),
            P(("groups", "tm"), None, None),
            P(("groups", "tm"), "chan", None),
        ),
        check_vma=False,
    )
```

```python
import math

import jax
import jax.numpy as jnp
import numpy as np
from jax import lax
from jax.experimental import pallas as pl
from jax.experimental.pallas import tpu as pltpu
from jax.sharding import PartitionSpec as P

DILATION_STEP = 2
PANEL = 32
GROUP = 8
LANES = 128
F32 = jnp.float32
BF16 = jnp.bfloat16

precise = lax.Precision.HIGHEST


def history(own, axis):
    count = lax.axis_size(axis)
    held = own
    reach = 1
    while reach < count:
        pairs = [(i, i + reach) for i in range(count - reach)]
        held = jnp.concatenate([held, lax.ppermute(held, axis, pairs)], axis=0)
        reach *= 2
    return held


def split(x):
    high = x.astype(BF16)
    return high, (x - high.astype(F32)).astype(BF16)


def contract(a, b, dims):
    return lax.dot_general(a, b, (dims, ((), ())), preferred_element_type=F32)


def three_pass(a, b, dims):
    return (
        contract(a[0], b[0], dims)
        + contract(a[0], b[1], dims)
        + contract(a[1], b[0], dims)
    )


NN = ((1,), (0,))
NT = ((1,), (1,))
TN = ((0,), (0,))


def prepare_kernel(
    transition, update_map, quiet_root, observed_root, init_root,
    map_high, map_low, grams, first_gram,
):
    for which, ref in ((0, transition), (1, update_map)):
        high, low = split(ref[...])
        map_high[which] = high
        map_low[which] = low
    for which, ref in ((0, quiet_root), (1, observed_root)):
        pair = split(ref[...])
        grams[which] = three_pass(pair, pair, TN)
    pair = split(init_root[...])
    first_gram[...] = three_pass(pair, pair, TN)


def prepare(transition, update_map, quiet_root, observed_root, init_root):
    size = transition.shape[0]
    return pl.pallas_call(
        prepare_kernel,
        out_shape=(
            jax.ShapeDtypeStruct((2, size, size), BF16),
            jax.ShapeDtypeStruct((2, size, size), BF16),
            jax.ShapeDtypeStruct((2, size, size), F32),
            jax.ShapeDtypeStruct((size, size), F32),
        ),
        name="prepare",
    )(transition, update_map, quiet_root, observed_root, init_root)


def upper_factor(gram, out, high, low):
    size = gram.shape[0]
    halves = size // LANES
    tile = (GROUP, LANES)
    zero = jnp.zeros(tile, F32)
    sub = lax.broadcasted_iota(jnp.int32, tile, 0)
    lane = lax.broadcasted_iota(jnp.int32, tile, 1)
    count = PANEL // GROUP
    for top in range(0, size, PANEL):
        first = top // LANES
        start = first * LANES
        panel = gram[top : top + PANEL, start:]
        if top:
            left = (high[:top, top : top + PANEL], low[:top, top : top + PANEL])
            panel = panel - three_pass(left, (high[:top, start:], low[:top, start:]), TN)
        places = range(halves - first)
        part = [
            [
                panel[GROUP * i : GROUP * (i + 1), LANES * h : LANES * (h + 1)]
                for h in places
            ]
            for i in range(count)
        ]
        done = [[zero for _ in places] for _ in range(count)]
        for g in range(count):
            base = top + GROUP * g
            here, at = base // LANES - first, base % LANES
            live = range(here, halves - first)
            column = {
                i: [
                    jnp.broadcast_to(part[i][here][:, at + j : at + j + 1], tile)
                    for j in range(GROUP)
                ]
                for i in range(g, count)
            }
            pivot = {
                (j, m): jnp.broadcast_to(column[g][m][j : j + 1, :], tile)
                for j in range(GROUP)
                for m in range(j, GROUP)
            }
            factor, scale = {}, []
            for j in range(GROUP):
                scale.append(lax.rsqrt(pivot[j, j]))
                for m in range(j + 1, GROUP):
                    factor[j, m] = pivot[j, m] * scale[j]
                for i in range(j + 1, GROUP):
                    for m in range(i, GROUP):
                        pivot[i, m] = pivot[i, m] - factor[j, i] * factor[j, m]
            rows = {}
            for h in live:
                rows[h] = []
                for j in range(GROUP):
                    value = jnp.broadcast_to(part[g][h][j : j + 1, :], tile)
                    for i in range(j):
                        value = value - factor[i, j] * rows[h][i]
                    rows[h].append(value * scale[j])
                value = rows[h][0]
                for j in range(1, GROUP):
                    value = jnp.where(sub == j, rows[h][j], value)
                if h == here:
                    value = jnp.where(lane - at >= sub, value, 0.0)
                done[g][h] = value
            for i in range(g + 1, count):
                left = []
                for j in range(GROUP):
                    value = column[i][j]
                    for m in range(j):
                        value = value - factor[m, j] * left[m]
                    left.append(value * scale[j])
                for h in live:
                    value = part[i][h]
                    for j in range(GROUP):
                        value = value - left[j] * rows[h][j]
                    part[i][h] = value
        for i in range(count):
            low_row = top + GROUP * i
            for h in range(halves):
                value = done[i][h - first] if h >= first else zero
                out[low_row : low_row + GROUP, LANES * h : LANES * (h + 1)] = value
        if top + PANEL < size:
            rows_high, rows_low = split(out[top : top + PANEL, :])
            high[top : top + PANEL, :] = rows_high
            low[top : top + PANEL, :] = rows_low


def covariance_kernel(steps, place, flags, map_high, map_low, grams, first_gram, out, gram, high, low):
    index = place[0]
    gram[...] = first_gram[...]

    def step(t, carry):
        flag = flags[(index - t // steps) * steps + t % steps]
        map_pair = (map_high[flag], map_low[flag])
        carried = three_pass(map_pair, split(gram[...]), NN)
        gram[...] = three_pass(split(carried), map_pair, NT) + grams[flag]
        return carry

    lax.fori_loop(0, (index + 1) * steps, step, 0)
    upper_factor(gram, out, high, low)


def covariance(place, flags, steps, map_high, map_low, grams, first_gram):
    size = first_gram.shape[0]
    vmem = pl.BlockSpec(memory_space=pltpu.VMEM)
    smem = pl.BlockSpec(memory_space=pltpu.SMEM)

    def kernel(*refs):
        covariance_kernel(steps, *refs)

    return pl.pallas_call(
        kernel,
        out_shape=jax.ShapeDtypeStruct((size, size), F32),
        in_specs=[smem, smem, vmem, vmem, vmem, vmem],
        out_specs=vmem,
        scratch_shapes=[
            pltpu.VMEM((size, size), F32),
            pltpu.VMEM((size, size), BF16),
            pltpu.VMEM((size, size), BF16),
        ],
        name="covariance",
    )(place, flags, map_high, map_low, grams, first_gram)


def means_kernel(steps, place, flags, map_high, map_low, shifts, init_mean, out):
    index = place[0]
    size = init_mean.shape[1]

    def step(t, mean):
        at = (index - t // steps) * steps + t % steps
        flag = flags[at]
        mean = three_pass(split(mean), (map_high[flag], map_low[flag]), NT)
        mean = mean + jnp.broadcast_to(shifts[pl.ds(at, 1), :], mean.shape)

        @pl.when(t // steps == index)
        def _():
            out[pl.ds(t % steps, 1), :] = mean[0:1]

        return mean

    lax.fori_loop(
        0, (index + 1) * steps, step, jnp.broadcast_to(init_mean[...], (GROUP, size))
    )


def means(place, flags, steps, map_high, map_low, shifts, init_mean):
    size = init_mean.shape[0]
    vmem = pl.BlockSpec(memory_space=pltpu.VMEM)
    smem = pl.BlockSpec(memory_space=pltpu.SMEM)

    def kernel(*refs):
        means_kernel(steps, *refs)

    return pl.pallas_call(
        kernel,
        out_shape=jax.ShapeDtypeStruct((steps, size), F32),
        in_specs=[smem, smem, vmem, vmem, vmem, vmem],
        out_specs=vmem,
        name="means",
    )(place, flags, map_high, map_low, shifts, init_mean[None])


LAGS = (0, DILATION_STEP, 2 * DILATION_STEP, -DILATION_STEP, -2 * DILATION_STEP)
TAPS = tuple((a, b) for a in (-1, 0, 1) for b in (-1, 0, 1))
EDGE = 2 * DILATION_STEP
KINDS = 8
EDGE_KINDS = 2
HALO_KINDS = 6


def moved(x, by, axis):
    if by == 0:
        return x
    length = x.shape[axis]
    shape = list(x.shape)
    shape[axis] = abs(by)
    zeros = jnp.zeros(shape, x.dtype)
    if by > 0:
        return jnp.concatenate(
            [lax.slice_in_dim(x, by, length, axis=axis), zeros], axis=axis
        )
    return jnp.concatenate(
        [zeros, lax.slice_in_dim(x, 0, length + by, axis=axis)], axis=axis
    )


def folded(x):
    total = x[:, :LANES]
    for at in range(LANES, x.shape[1], LANES):
        total = total + x[:, at : at + LANES]
    return total


def frames_kernel(taps, flags, frames, pooling, part, stats, pooled):
    steps, block, rows, columns = frames.shape
    first = pl.program_id(0) * block

    @pl.when(pl.program_id(0) == 0)
    def _():
        for k, (a, b) in enumerate(TAPS):
            pooled[k] = moved(
                moved(pooling[...], -DILATION_STEP * b, 1), -DILATION_STEP * a, 0
            )

    lane = lax.broadcasted_iota(jnp.int32, (rows, LANES), 1)
    row = lax.broadcasted_iota(jnp.int32, (rows, LANES), 0)
    masks = [lax.rem(lane, rows) - row == lag for lag in LAGS]
    right_masks = [(lane - row == lag) & (lane < rows) for lag in LAGS[:3]]
    column = lax.broadcasted_iota(jnp.int32, (rows, columns), 1)
    left_edge = (column < DILATION_STEP).astype(F32).astype(BF16)
    right_edge = (column >= columns - DILATION_STEP).astype(F32).astype(BF16)
    blank = jnp.zeros((rows, 2 * LANES - 5 * rows), F32)
    for c in range(block):
        weights = taps[first + c, 0] * pooled[0]
        for k in range(1, len(TAPS)):
            weights = weights + taps[first + c, k] * pooled[k]
        gram = jnp.zeros((rows, 5 * rows), F32)
        for t in range(steps):
            frame = frames[t, c]
            part[t, c : c + 1, :] = jnp.sum(
                folded(frame.astype(F32) * weights), axis=0, keepdims=True
            )
            partners = jnp.concatenate(
                [
                    frame,
                    moved(frame, DILATION_STEP, 1),
                    moved(frame, 2 * DILATION_STEP, 1),
                    frame * left_edge,
                    frame * right_edge,
                ],
                axis=0,
            )
            gram = gram + contract(frame * flags[t].astype(F32).astype(BF16), partners, NT)
        near = gram[:, :LANES]
        far = jnp.concatenate([gram[:, LANES:], blank], axis=1)
        sums = [jnp.sum(jnp.where(m, near, 0.0), axis=0, keepdims=True) for m in masks]
        sums += [jnp.sum(jnp.where(m, far, 0.0), axis=0, keepdims=True) for m in right_masks]
        stats[c : c + 1, :] = jnp.concatenate(sums, axis=1)


def frame_sums(taps, flags, frames, pooling):
    steps, channels, rows, columns = frames.shape
    block = math.gcd(channels, 16)
    vmem = pl.BlockSpec(memory_space=pltpu.VMEM)
    smem = pl.BlockSpec(memory_space=pltpu.SMEM)
    return pl.pallas_call(
        frames_kernel,
        grid=(channels // block,),
        out_shape=(
            jax.ShapeDtypeStruct((steps, channels, LANES), F32),
            jax.ShapeDtypeStruct((channels, KINDS * LANES), F32),
        ),
        in_specs=[
            smem,
            smem,
            pl.BlockSpec((steps, block, rows, columns), lambda i: (0, i, 0, 0)),
            vmem,
        ],
        out_specs=(
            pl.BlockSpec((steps, block, LANES), lambda i: (0, i, 0)),
            pl.BlockSpec((block, KINDS * LANES), lambda i: (i, 0)),
        ),
        scratch_shapes=[pltpu.VMEM((len(TAPS), rows, columns), F32)],
        name="frame_sums",
    )(taps, flags, frames, pooling)


def selection(rows):
    near = np.zeros((KINDS, LANES, len(TAPS), len(TAPS)), np.float32)
    edge = np.zeros((EDGE_KINDS, LANES, len(TAPS), len(TAPS)), np.float32)
    halo = np.zeros((2, HALO_KINDS, LANES, len(TAPS), len(TAPS)), np.float32)
    own = np.arange(rows)
    top, bottom = own[:DILATION_STEP], own[rows - DILATION_STEP :]
    for i, (a, b) in enumerate(TAPS):
        for j, (c, d) in enumerate(TAPS):
            down, across = c - a, d - b
            if (down, across) < (0, 0):
                down, across = -down, -across
            lag = abs(across)
            kind = down if across >= 0 else down + 2
            near[kind, lag * rows + own, i, j] += 1
            if down:
                if across == 0:
                    halo[down - 1, :2, :, i, j] += 1
                else:
                    halo[down - 1, 1 + lag + (2 if across < 0 else 0), :, i, j] += 1
            if b == d == 1:
                near[down, 3 * rows + own, i, j] -= 1
                if down:
                    halo[down - 1, 0, :DILATION_STEP, i, j] -= 1
            if b == d == -1:
                near[5 + down, own, i, j] -= 1
                if down:
                    halo[down - 1, 1, LANES - DILATION_STEP :, i, j] -= 1
            if a == c != 0:
                lost = top if a == 1 else bottom
                edge[0, lag * rows + lost, i, j] -= 1
                if b == d == 1:
                    edge[0, 3 * rows + lost, i, j] += 1
                if b == d == -1:
                    edge[1, lost, i, j] += 1
    pairs = len(TAPS) ** 2
    table = np.concatenate([m.reshape(-1, pairs) for m in (near, edge, halo)], axis=0)
    return np.pad(table, ((0, 0), (0, LANES - pairs)))


def finish_kernel(
    scale, flags, edges, above, below, part, stats, taps, pooling, gain, table,
    gain_part, gradient, values,
):
    steps, _, channels, columns = edges.shape
    rows = pooling.shape[0]
    place, count = lax.axis_index("space"), lax.axis_size("space")
    has_above = jnp.where(place > 0, 1.0, 0.0).astype(F32)
    has_below = jnp.where(place < count - 1, 1.0, 0.0).astype(F32)
    halo_weights = []
    for side, (a, start, has) in enumerate(
        ((-1, 0, has_above), (1, rows - DILATION_STEP, has_below))
    ):
        for r in range(DILATION_STEP):
            value = jnp.zeros((channels, columns), F32)
            for b in (-1, 0, 1):
                k = TAPS.index((a, b))
                shifted = moved(pooling[start + r : start + r + 1, :], -DILATION_STEP * b, 1)
                value = value + taps[:, k : k + 1] * shifted
            halo_weights.append(value * has)
    sums = [[None] * 5 for _ in range(2)]
    ones = jnp.ones((GROUP, LANES), BF16)
    row_sums = []
    for t in range(steps):
        flag = flags[t].astype(F32)
        upper = [above[t, r].astype(F32) for r in range(DILATION_STEP)]
        lower = [below[t, r].astype(F32) for r in range(DILATION_STEP)]
        total = jnp.zeros((channels, columns), F32)
        for value, weight in zip(upper + lower, halo_weights):
            total = total + value * weight
        row_sums.append(part[t] + folded(total))
        for r in range(DILATION_STEP):
            near_top = edges[t, DILATION_STEP + r].astype(F32)
            far_bottom = edges[t, 2 * DILATION_STEP + r].astype(F32)
            near_bottom = edges[t, 3 * DILATION_STEP + r].astype(F32)
            high, low = upper[r] * (flag * has_above), lower[r] * (flag * has_below)
            for n in range(-2, 3):
                shifted_low = moved(low, DILATION_STEP * n, 1)
                shifted_high = moved(high, -DILATION_STEP * n, 1)
                one = near_bottom * shifted_low
                two = far_bottom * shifted_low + near_top * shifted_high
                for which, value in ((0, one), (1, two)):
                    old = sums[which][n]
                    sums[which][n] = value if old is None else old + value
    high, low = split(jnp.concatenate(row_sums, axis=0))
    tile_sums = contract(ones, high, NT) + contract(ones, low, NT)
    shape = (GROUP, steps * channels)
    owner = lax.broadcasted_iota(jnp.int32, shape, 1) // channels
    step = lax.broadcasted_iota(jnp.int32, shape, 0)
    seen = jnp.zeros(shape, F32)
    for t in range(steps):
        seen = jnp.where((owner == t) & (step == t), flags[t].astype(F32), seen)
    gains = jnp.concatenate([gain[...]] * steps, axis=1)
    product = three_pass(split(tile_sums * seen), split(gains), NT)
    gain_part[...] = product[:steps]
    values[:, : KINDS * LANES] = stats[...]
    lane = lax.broadcasted_iota(jnp.int32, (channels, LANES), 1) % rows
    outside = jnp.where(lane < DILATION_STEP, 1.0 - has_above, 0.0)
    outside = jnp.where(lane >= rows - DILATION_STEP, 1.0 - has_below, outside)
    at = KINDS * LANES
    for kind in (0, 5):
        values[:, at : at + LANES] = stats[:, kind * LANES : (kind + 1) * LANES] * outside
        at += LANES
    for which in range(2):
        centre = sums[which][0]
        pieces = [centre[:, :LANES], centre[:, columns - LANES :]]
        for inner in range(LANES, columns - LANES, LANES):
            pieces[2] = pieces[2] + centre[:, inner : inner + LANES]
        pieces += [folded(sums[which][n]) for n in (1, 2, -1, -2)]
        for piece in pieces:
            values[:, at : at + LANES] = piece
            at += LANES
    high, low = split(values[...])
    pairs = contract(high, table[...], NN) + contract(low, table[...], NN)
    tap_count = len(TAPS)
    source = lax.broadcasted_iota(jnp.int32, (tap_count, LANES), 1)
    spread_row = lax.broadcasted_iota(jnp.int32, (tap_count, LANES), 0)
    spread = (source // tap_count == spread_row).astype(F32)
    pair = lax.broadcasted_iota(jnp.int32, (LANES, LANES), 0)
    target = lax.broadcasted_iota(jnp.int32, (LANES, LANES), 1)
    gather = (pair % tap_count == target).astype(F32)
    weights = jnp.dot(taps[...], spread, precision=precise, preferred_element_type=F32)
    result = jnp.dot(pairs * weights, gather, precision=precise, preferred_element_type=F32)
    gradient[...] = result * scale


def finish(flags, edges, above, below, part, stats, taps, pooling, gain):
    steps, _, channels, columns = edges.shape
    rows = pooling.shape[0]
    scale = 1.0 / (rows * lax.axis_size("space") * columns)
    table = jnp.asarray(selection(rows), BF16)
    vmem = pl.BlockSpec(memory_space=pltpu.VMEM)
    smem = pl.BlockSpec(memory_space=pltpu.SMEM)

    def kernel(*refs):
        finish_kernel(scale, *refs)

    return pl.pallas_call(
        kernel,
        out_shape=(
            jax.ShapeDtypeStruct((steps, gain.shape[0]), F32),
            jax.ShapeDtypeStruct((channels, LANES), F32),
        ),
        in_specs=[smem] + [vmem] * 9,
        out_specs=(vmem, vmem),
        scratch_shapes=[pltpu.VMEM((channels, table.shape[0]), F32)],
        name="finish",
    )(flags, edges, above, below, part, stats, taps, pooling, gain, table)


def beside(edges, axis):
    count = lax.axis_size(axis)
    top = edges[:, :DILATION_STEP]
    bottom = edges[:, -DILATION_STEP:]
    if count == 2:
        sent = jnp.where(lax.axis_index(axis) == 0, bottom, top)
        got = lax.ppermute(sent, axis, [(0, 1), (1, 0)])
        return got, got
    forward = [(i, (i + 1) % count) for i in range(count)]
    backward = [(target, source) for source, target in forward]
    return lax.ppermute(bottom, axis, forward), lax.ppermute(top, axis, backward)


def total(value, axis):
    if lax.axis_size(axis) == 2:
        return value + lax.ppermute(value, axis, [(0, 1), (1, 0)])
    return lax.psum(value, axis)


def local(
    frames,
    conv_taps,
    pooling,
    gain_matrix,
    transition,
    update_map,
    quiet_root,
    observed_root,
    init_mean,
    init_root,
    observed,
):
    step_count, channels, rows, columns = frames.shape
    place = lax.axis_index("tm").astype(jnp.int32)[None]
    edges = jnp.concatenate([frames[:, :, :EDGE], frames[:, :, rows - EDGE :]], axis=2)
    edges = edges.transpose(0, 2, 1, 3)
    above, below = beside(edges, "space")
    flags = history(observed, "tm")
    part, stats = frame_sums(conv_taps, observed, frames, pooling)
    map_high, map_low, grams, first_gram = prepare(
        transition, update_map, quiet_root, observed_root, init_root
    )
    gain_part, gradient = finish(
        observed, edges, above, below, part, stats, conv_taps, pooling, gain_matrix
    )
    shifts = total(total(gain_part, "chan"), "space")
    gradient = total(gradient, "space")
    all_shifts = history(shifts, "tm")
    root = covariance(place, flags, step_count, map_high, map_low, grams, first_gram)
    filtered_means = means(place, flags, step_count, map_high, map_low, all_shifts, init_mean)
    return (filtered_means, root[None], gradient[None, :, : len(TAPS)])


def solution(mesh):
    return jax.shard_map(
        local,
        mesh=mesh,
        in_specs=(
            P(("groups", "tm"), "chan", "space", None),
            P("chan", None),
            P("space", None),
            P(None, ("space", "chan")),
            P(),
            P(),
            P(),
            P(),
            P("groups"),
            P("groups", None),
            P(("groups", "tm")),
        ),
        out_specs=(
            P(("groups", "tm"), None),
            P(("groups", "tm"), None, None),
            P(("groups", "tm"), "chan", None),
        ),
        check_vma=False,
    )
```

```python
import math

import jax
import jax.numpy as jnp
import numpy as np
from jax import lax
from jax.experimental import pallas as pl
from jax.experimental.pallas import tpu as pltpu
from jax.sharding import PartitionSpec as P


DILATION_STEP = 2
PANEL = 32
GROUP = 8
LANES = 128
F32 = jnp.float32
BF16 = jnp.bfloat16

precise = lax.Precision.HIGHEST


def history(own, axis):
    count = lax.axis_size(axis)
    if count <= 4:
        held = [own]
        for lag in range(1, count):
            ring = [(i, (i + lag) % count) for i in range(count)]
            held.append(lax.ppermute(own, axis, ring))
        return jnp.concatenate(held, axis=0)
    held = own
    reach = 1
    while reach < count:
        pairs = [(i, i + reach) for i in range(count - reach)]
        held = jnp.concatenate([held, lax.ppermute(held, axis, pairs)], axis=0)
        reach *= 2
    return held


def split(x):
    high = x.astype(BF16)
    return high, (x - high.astype(F32)).astype(BF16)


def contract(a, b, dims):
    return lax.dot_general(a, b, (dims, ((), ())), preferred_element_type=F32)


def three_pass(a, b, dims):
    return (
        contract(a[0], b[0], dims)
        + contract(a[0], b[1], dims)
        + contract(a[1], b[0], dims)
    )


def exact(a, b, dims):
    return lax.dot_general(
        a, b, (dims, ((), ())), precision=precise, preferred_element_type=F32
    )


NN = ((1,), (0,))
NT = ((1,), (1,))
TN = ((0,), (0,))


def prepare_kernel(
    transition, update_map, quiet_root, observed_root, init_root,
    map_high, map_low, grams, first_gram,
):
    for which, ref in enumerate((transition, update_map)):
        map_high[which], map_low[which] = split(ref[...])
    for which, ref in enumerate((quiet_root, observed_root)):
        pair = split(ref[...])
        grams[which] = three_pass(pair, pair, TN)
    pair = split(init_root[...])
    first_gram[...] = three_pass(pair, pair, TN)


def prepare(transition, update_map, quiet_root, observed_root, init_root):
    size = transition.shape[0]
    return pl.pallas_call(
        prepare_kernel,
        out_shape=(
            jax.ShapeDtypeStruct((2, size, size), BF16),
            jax.ShapeDtypeStruct((2, size, size), BF16),
            jax.ShapeDtypeStruct((2, size, size), F32),
            jax.ShapeDtypeStruct((size, size), F32),
        ),
        name="prepare",
    )(transition, update_map, quiet_root, observed_root, init_root)


def pairs_kernel(map_high, map_low, grams, pair_high, pair_low, pair_gram):
    maps = [(map_high[which], map_low[which]) for which in range(2)]
    for later in range(2):
        for earlier in range(2):
            which = 2 * later + earlier
            joined = three_pass(maps[later], maps[earlier], NN)
            pair_high[which], pair_low[which] = split(joined)
            carried = three_pass(maps[later], split(grams[earlier]), NN)
            pair_gram[which] = three_pass(split(carried), maps[later], NT) + grams[later]


def pair_maps(map_high, map_low, grams):
    size = grams.shape[1]
    return pl.pallas_call(
        pairs_kernel,
        out_shape=(
            jax.ShapeDtypeStruct((4, size, size), BF16),
            jax.ShapeDtypeStruct((4, size, size), BF16),
            jax.ShapeDtypeStruct((4, size, size), F32),
        ),
        name="pair_maps",
    )(map_high, map_low, grams)


def upper_factor(gram, out, high, low, beside_work=()):
    size = gram.shape[0]
    halves = size // LANES
    tile = (GROUP, LANES)
    zero = jnp.zeros(tile, F32)
    sub = lax.broadcasted_iota(jnp.int32, tile, 0)
    lane = lax.broadcasted_iota(jnp.int32, tile, 1)
    count = PANEL // GROUP
    pending = list(beside_work)
    for top in range(0, size, PANEL):
        first = top // LANES
        start = first * LANES
        panel = gram[top : top + PANEL, start:]
        if top:
            left = (high[:top, top : top + PANEL], low[:top, top : top + PANEL])
            panel = panel - three_pass(left, (high[:top, start:], low[:top, start:]), TN)
        places = range(halves - first)
        part = [
            [
                panel[GROUP * i : GROUP * (i + 1), LANES * h : LANES * (h + 1)]
                for h in places
            ]
            for i in range(count)
        ]
        done = [[zero for _ in places] for _ in range(count)]
        for g in range(count):
            if pending:
                pending.pop(0)()
            base = top + GROUP * g
            here, at = base // LANES - first, base % LANES
            live = range(here, halves - first)
            column = {
                i: [
                    jnp.broadcast_to(part[i][here][:, at + j : at + j + 1], tile)
                    for j in range(GROUP)
                ]
                for i in range(g, count)
            }
            pivot = {
                (j, m): jnp.broadcast_to(column[g][m][j : j + 1, :], tile)
                for j in range(GROUP)
                for m in range(j, GROUP)
            }
            factor, scale = {}, []
            for j in range(GROUP):
                scale.append(lax.rsqrt(pivot[j, j]))
                for m in range(j + 1, GROUP):
                    factor[j, m] = pivot[j, m] * scale[j]
                for i in range(j + 1, GROUP):
                    for m in range(i, GROUP):
                        pivot[i, m] = pivot[i, m] - factor[j, i] * factor[j, m]
            rows = {}
            for h in live:
                rows[h] = []
                for j in range(GROUP):
                    value = jnp.broadcast_to(part[g][h][j : j + 1, :], tile)
                    for i in range(j):
                        value = value - factor[i, j] * rows[h][i]
                    rows[h].append(value * scale[j])
                value = rows[h][0]
                for j in range(1, GROUP):
                    value = jnp.where(sub == j, rows[h][j], value)
                if h == here:
                    value = jnp.where(lane - at >= sub, value, 0.0)
                done[g][h] = value
            for i in range(g + 1, count):
                left = []
                for j in range(GROUP):
                    value = column[i][j]
                    for m in range(j):
                        value = value - factor[m, j] * left[m]
                    left.append(value * scale[j])
                for h in live:
                    value = part[i][h]
                    for j in range(GROUP):
                        value = value - left[j] * rows[h][j]
                    part[i][h] = value
        for i in range(count):
            low_row = top + GROUP * i
            for h in range(halves):
                value = done[i][h - first] if h >= first else zero
                out[low_row : low_row + GROUP, LANES * h : LANES * (h + 1)] = value
        if top + PANEL < size:
            rows_high, rows_low = split(out[top : top + PANEL, :])
            high[top : top + PANEL, :] = rows_high
            low[top : top + PANEL, :] = rows_low
    for work in pending:
        work()


def recursion_kernel(steps, span, place, flags, span_high, span_low, span_gram, first_gram, gram):
    index = place[0]
    pieces = steps // span
    gram[...] = first_gram[...]

    def step(n, carry):
        at = (index - n // pieces) * steps + (n % pieces) * span
        which = flags[at]
        for later in range(1, span):
            which = which + flags[at + later] * 2**later
        map_pair = (span_high[which], span_low[which])
        carried = three_pass(map_pair, split(gram[...]), NN)
        gram[...] = three_pass(split(carried), map_pair, NT) + span_gram[which]
        return carry

    lax.fori_loop(0, (index + 1) * pieces, step, 0)


def recursion(place, flags, steps, span, span_high, span_low, span_gram, first_gram):
    vmem = pl.BlockSpec(memory_space=pltpu.VMEM)
    smem = pl.BlockSpec(memory_space=pltpu.SMEM)

    def kernel(*refs):
        recursion_kernel(steps, span, *refs)

    return pl.pallas_call(
        kernel,
        out_shape=jax.ShapeDtypeStruct(first_gram.shape, F32),
        in_specs=[smem, smem, vmem, vmem, vmem, vmem],
        out_specs=vmem,
        name="recursion",
    )(place, flags, span_high, span_low, span_gram, first_gram)


def factor_kernel(
    steps, span, place, flags, gram, map_high, map_low, span_high, span_low, shifts, init_mean,
    out, mean_out, high, low, carried,
):
    index = place[0]
    size = gram.shape[0]
    blocks = shifts.shape[0]
    state = {"mean": jnp.broadcast_to(init_mean[...], (GROUP, size))}

    def first():
        rows = split(jnp.concatenate([shifts[block] for block in range(blocks)], axis=0))
        for which in range(2):
            carried[which] = three_pass(rows, (map_high[which], map_low[which]), NT)

    def one_step(block, t):
        at = block * steps + t
        flag = flags[at]
        mean = three_pass(split(state["mean"]), (map_high[flag], map_low[flag]), NT)
        return mean + shifts[block, t : t + 1, :]

    def work(block, t):
        def run():
            if block == 0:
                mean = one_step(block, t)
                mean_out[t : t + 1, :] = mean[0:1]
                if span == 1:
                    state["mean"] = mean
                    return
            if span == 1:
                mean = one_step(block, t)
            else:
                at = block * steps + t
                which = flags[at] + 2 * flags[at + 1]
                mean = three_pass(split(state["mean"]), (span_high[which], span_low[which]), NT)
                row = block * shifts.shape[1] + t
                mean = mean + carried[flags[at + 1], row : row + 1, :]
                mean = mean + shifts[block, t + 1 : t + 2, :]
                if block == 0:
                    mean_out[t + 1 : t + 2, :] = mean[0:1]
            state["mean"] = mean if block == 0 else jnp.where(block <= index, mean, state["mean"])

        return run

    jobs = [first] if span == 2 else []
    jobs += [work(block, t) for block in reversed(range(blocks)) for t in range(0, steps, span)]
    upper_factor(gram, out, high, low, jobs)


def factor(
    place, flags, steps, span, gram, map_high, map_low, span_high, span_low, shifts, init_mean
):
    size = gram.shape[0]
    vmem = pl.BlockSpec(memory_space=pltpu.VMEM)
    smem = pl.BlockSpec(memory_space=pltpu.SMEM)

    def kernel(*refs):
        factor_kernel(steps, span, *refs)

    return pl.pallas_call(
        kernel,
        out_shape=(
            jax.ShapeDtypeStruct((size, size), F32),
            jax.ShapeDtypeStruct((steps, size), F32),
        ),
        in_specs=[smem, smem] + [vmem] * 7,
        out_specs=(vmem, vmem),
        scratch_shapes=[
            pltpu.VMEM((size, size), BF16),
            pltpu.VMEM((size, size), BF16),
            pltpu.VMEM((2, shifts.shape[0] * shifts.shape[1], size), F32),
        ],
        name="factor",
    )(place, flags, gram, map_high, map_low, span_high, span_low, shifts, init_mean[None])


LAGS = (0, DILATION_STEP, 2 * DILATION_STEP, -DILATION_STEP, -2 * DILATION_STEP)
TAPS = tuple((a, b) for a in (-1, 0, 1) for b in (-1, 0, 1))
EDGE = 2 * DILATION_STEP
KINDS = 8
EDGE_KINDS = 2
HALO_KINDS = 6


def moved(x, by, axis):
    if by == 0:
        return x
    length = x.shape[axis]
    shape = list(x.shape)
    shape[axis] = abs(by)
    zeros = jnp.zeros(shape, x.dtype)
    if by > 0:
        return jnp.concatenate(
            [lax.slice_in_dim(x, by, length, axis=axis), zeros], axis=axis
        )
    return jnp.concatenate(
        [zeros, lax.slice_in_dim(x, 0, length + by, axis=axis)], axis=axis
    )


def folded(x):
    total = x[:, :LANES]
    for at in range(LANES, x.shape[1], LANES):
        total = total + x[:, at : at + LANES]
    return total


def frames_kernel(taps, flags, frames, pooling, part, stats, pooled):
    steps, block, rows, columns = frames.shape
    first = pl.program_id(0) * block

    @pl.when(pl.program_id(0) == 0)
    def _():
        for k, (a, b) in enumerate(TAPS):
            pooled[k] = moved(
                moved(pooling[...], -DILATION_STEP * b, 1), -DILATION_STEP * a, 0
            )

    lane = lax.broadcasted_iota(jnp.int32, (rows, LANES), 1)
    row = lax.broadcasted_iota(jnp.int32, (rows, LANES), 0)
    masks = [lax.rem(lane, rows) - row == lag for lag in LAGS]
    right_masks = [(lane - row == lag) & (lane < rows) for lag in LAGS[:3]]
    column = lax.broadcasted_iota(jnp.int32, (rows, columns), 1)
    left_edge = (column < DILATION_STEP).astype(F32).astype(BF16)
    right_edge = (column >= columns - DILATION_STEP).astype(F32).astype(BF16)
    blank = jnp.zeros((rows, 2 * LANES - 5 * rows), F32)
    for c in range(block):
        weights = taps[0, first + c] * pooled[0]
        for k in range(1, len(TAPS)):
            weights = weights + taps[k, first + c] * pooled[k]
        gram = jnp.zeros((rows, 5 * rows), F32)
        for t in range(steps):
            frame = frames[t, c]
            part[t, c : c + 1, :] = jnp.sum(
                folded(frame.astype(F32) * weights), axis=0, keepdims=True
            )
            partners = jnp.concatenate(
                [
                    frame,
                    moved(frame, DILATION_STEP, 1),
                    moved(frame, 2 * DILATION_STEP, 1),
                    frame * left_edge,
                    frame * right_edge,
                ],
                axis=0,
            )
            gram = gram + contract(frame * flags[t].astype(F32).astype(BF16), partners, NT)
        near = gram[:, :LANES]
        far = jnp.concatenate([gram[:, LANES:], blank], axis=1)
        sums = [jnp.sum(jnp.where(m, near, 0.0), axis=0, keepdims=True) for m in masks]
        sums += [jnp.sum(jnp.where(m, far, 0.0), axis=0, keepdims=True) for m in right_masks]
        stats[c : c + 1, :] = jnp.concatenate(sums, axis=1)


def frame_sums(taps, flags, frames, pooling):
    steps, channels, rows, columns = frames.shape
    block = math.gcd(channels, 16)
    vmem = pl.BlockSpec(memory_space=pltpu.VMEM)
    smem = pl.BlockSpec(memory_space=pltpu.SMEM)
    return pl.pallas_call(
        frames_kernel,
        grid=(channels // block,),
        out_shape=(
            jax.ShapeDtypeStruct((steps, channels, LANES), F32),
            jax.ShapeDtypeStruct((channels, KINDS * LANES), F32),
        ),
        in_specs=[
            smem,
            smem,
            pl.BlockSpec((steps, block, rows, columns), lambda i: (0, i, 0, 0)),
            vmem,
        ],
        out_specs=(
            pl.BlockSpec((steps, block, LANES), lambda i: (0, i, 0)),
            pl.BlockSpec((block, KINDS * LANES), lambda i: (i, 0)),
        ),
        scratch_shapes=[pltpu.VMEM((len(TAPS), rows, columns), F32)],
        name="frame_sums",
    )(taps, flags, frames, pooling)


def selection(rows):
    near = np.zeros((KINDS, LANES, len(TAPS), len(TAPS)), np.float32)
    edge = np.zeros((EDGE_KINDS, LANES, len(TAPS), len(TAPS)), np.float32)
    halo = np.zeros((2, HALO_KINDS, LANES, len(TAPS), len(TAPS)), np.float32)
    own = np.arange(rows)
    top, bottom = own[:DILATION_STEP], own[rows - DILATION_STEP :]
    for i, (a, b) in enumerate(TAPS):
        for j, (c, d) in enumerate(TAPS):
            down, across = c - a, d - b
            if (down, across) < (0, 0):
                down, across = -down, -across
            lag = abs(across)
            kind = down if across >= 0 else down + 2
            near[kind, lag * rows + own, i, j] += 1
            if down:
                if across == 0:
                    halo[down - 1, :2, :, i, j] += 1
                else:
                    halo[down - 1, 1 + lag + (2 if across < 0 else 0), :, i, j] += 1
            if b == d == 1:
                near[down, 3 * rows + own, i, j] -= 1
                if down:
                    halo[down - 1, 0, :DILATION_STEP, i, j] -= 1
            if b == d == -1:
                near[5 + down, own, i, j] -= 1
                if down:
                    halo[down - 1, 1, LANES - DILATION_STEP :, i, j] -= 1
            if a == c != 0:
                lost = top if a == 1 else bottom
                edge[0, lag * rows + lost, i, j] -= 1
                if b == d == 1:
                    edge[0, 3 * rows + lost, i, j] += 1
                if b == d == -1:
                    edge[1, lost, i, j] += 1
    pairs = len(TAPS) ** 2
    table = np.concatenate([m.reshape(-1, pairs) for m in (near, edge, halo)], axis=0)
    return np.pad(table, ((0, 0), (0, LANES - pairs)))


def beside_tile():
    place, count = lax.axis_index("space"), lax.axis_size("space")
    has_above = jnp.where(place > 0, 1.0, 0.0).astype(F32)
    has_below = jnp.where(place < count - 1, 1.0, 0.0).astype(F32)
    return has_above, has_below


def spread():
    shape = (len(TAPS), LANES)
    source = lax.broadcasted_iota(jnp.int32, shape, 1)
    return source, lax.broadcasted_iota(jnp.int32, shape, 0)


def gain_kernel(flags, above, below, part, taps, pooling, gain, gain_part):
    steps, _, channels, columns = above.shape
    rows = pooling.shape[0]
    has_above, has_below = beside_tile()
    source, tap = spread()
    tap_columns = exact(taps[...], (source == tap).astype(F32), TN)
    halo_weights = []
    for a, start, has in ((-1, 0, has_above), (1, rows - DILATION_STEP, has_below)):
        for r in range(DILATION_STEP):
            value = jnp.zeros((channels, columns), F32)
            for b in (-1, 0, 1):
                k = TAPS.index((a, b))
                shifted = moved(pooling[start + r : start + r + 1, :], -DILATION_STEP * b, 1)
                value = value + tap_columns[:, k : k + 1] * shifted
            halo_weights.append(value * has)
    row_sums = []
    for t in range(steps):
        total = jnp.zeros((channels, columns), F32)
        for r in range(DILATION_STEP):
            total = total + above[t, r].astype(F32) * halo_weights[r]
            total = total + below[t, r].astype(F32) * halo_weights[DILATION_STEP + r]
        row_sums.append(part[t] + folded(total))
    ones = jnp.ones((GROUP, LANES), BF16)
    high, low = split(jnp.concatenate(row_sums, axis=0))
    tile_sums = contract(ones, high, NT) + contract(ones, low, NT)
    shape = (GROUP, steps * channels)
    owner = lax.broadcasted_iota(jnp.int32, shape, 1) // channels
    step = lax.broadcasted_iota(jnp.int32, shape, 0)
    seen = jnp.zeros(shape, F32)
    for t in range(steps):
        seen = jnp.where((owner == t) & (step == t), flags[t].astype(F32), seen)
    gains = jnp.concatenate([gain[...]] * steps, axis=0)
    product = three_pass(split(tile_sums * seen), split(gains), NN)
    gain_part[...] = product[:steps]


def gain_sums(flags, above, below, part, taps, pooling, gain):
    vmem = pl.BlockSpec(memory_space=pltpu.VMEM)
    smem = pl.BlockSpec(memory_space=pltpu.SMEM)
    return pl.pallas_call(
        gain_kernel,
        out_shape=jax.ShapeDtypeStruct((above.shape[0], gain.shape[1]), F32),
        in_specs=[smem] + [vmem] * 6,
        out_specs=vmem,
        name="gain_sums",
    )(flags, above, below, part, taps, pooling, gain)


def gradient_kernel(
    scale, rows, flags, edges, above, below, stats, taps, table, gradient, values
):
    steps, _, channels, columns = edges.shape
    has_above, has_below = beside_tile()
    sums = [[None] * 5 for _ in range(2)]
    for t in range(steps):
        flag = flags[t].astype(F32)
        for r in range(DILATION_STEP):
            near_top = edges[t, DILATION_STEP + r].astype(F32)
            far_bottom = edges[t, 2 * DILATION_STEP + r].astype(F32)
            near_bottom = edges[t, 3 * DILATION_STEP + r].astype(F32)
            high = above[t, r].astype(F32) * (flag * has_above)
            low = below[t, r].astype(F32) * (flag * has_below)
            for n in range(-2, 3):
                shifted_low = moved(low, DILATION_STEP * n, 1)
                shifted_high = moved(high, -DILATION_STEP * n, 1)
                one = near_bottom * shifted_low
                two = far_bottom * shifted_low + near_top * shifted_high
                for which, value in ((0, one), (1, two)):
                    old = sums[which][n]
                    sums[which][n] = value if old is None else old + value
    values[:, : KINDS * LANES] = stats[...]
    lane = lax.rem(lax.broadcasted_iota(jnp.int32, (channels, LANES), 1), rows)
    outside = jnp.where(lane < DILATION_STEP, 1.0 - has_above, 0.0)
    outside = jnp.where(lane >= rows - DILATION_STEP, 1.0 - has_below, outside)
    at = KINDS * LANES
    for kind in (0, 5):
        values[:, at : at + LANES] = stats[:, kind * LANES : (kind + 1) * LANES] * outside
        at += LANES
    for which in range(2):
        centre = sums[which][0]
        pieces = [centre[:, :LANES], centre[:, columns - LANES :]]
        pieces += [folded(sums[which][n]) for n in (1, 2, -1, -2)]
        for inner in range(LANES, columns - LANES, LANES):
            middle = jnp.sum(centre[:, inner : inner + LANES], axis=1, keepdims=True)
            pieces[0] = pieces[0] + jnp.where(lane_of(channels) == LANES // 2, middle, 0.0)
        for piece in pieces:
            values[:, at : at + LANES] = piece
            at += LANES
    high, low = split(values[...])
    pairs = contract(high, table[...], NN) + contract(low, table[...], NN)
    source, tap = spread()
    weights = exact(taps[...], (source // len(TAPS) == tap).astype(F32), TN)
    gathered = (source % len(TAPS) == tap).astype(F32)
    gradient[...] = exact(gathered, pairs * weights, NT) * scale


def lane_of(channels):
    return lax.broadcasted_iota(jnp.int32, (channels, LANES), 1)


def tap_sums(flags, edges, above, below, stats, taps, rows):
    _, _, channels, columns = edges.shape
    scale = 1.0 / (rows * lax.axis_size("space") * columns)
    table = jnp.asarray(selection(rows), BF16)
    vmem = pl.BlockSpec(memory_space=pltpu.VMEM)
    smem = pl.BlockSpec(memory_space=pltpu.SMEM)

    def kernel(*refs):
        gradient_kernel(scale, rows, *refs)

    return pl.pallas_call(
        kernel,
        out_shape=jax.ShapeDtypeStruct((len(TAPS), channels), F32),
        in_specs=[smem] + [vmem] * 6,
        out_specs=vmem,
        scratch_shapes=[pltpu.VMEM((channels, table.shape[0]), F32)],
        name="tap_sums",
    )(flags, edges, above, below, stats, taps, table)


def beside(edges, axis):
    count = lax.axis_size(axis)
    top = edges[:, :DILATION_STEP]
    bottom = edges[:, -DILATION_STEP:]
    if count == 2:
        sent = jnp.where(lax.axis_index(axis) == 0, bottom, top)
        got = lax.ppermute(sent, axis, [(0, 1), (1, 0)])
        return got, got
    forward = [(i, (i + 1) % count) for i in range(count)]
    backward = [(target, source) for source, target in forward]
    return lax.ppermute(bottom, axis, forward), lax.ppermute(top, axis, backward)


def total(value, axis):
    if lax.axis_size(axis) == 2:
        return value + lax.ppermute(value, axis, [(0, 1), (1, 0)])
    return lax.psum(value, axis)


def local(
    frames,
    conv_taps,
    pooling,
    gain_matrix,
    transition,
    update_map,
    quiet_root,
    observed_root,
    init_mean,
    init_root,
    observed,
):
    step_count, _, rows, _ = frames.shape
    place = lax.axis_index("tm").astype(jnp.int32)[None]
    edges = jnp.concatenate([frames[:, :, :EDGE], frames[:, :, rows - EDGE :]], axis=2)
    edges = edges.transpose(0, 2, 1, 3)
    above, below = beside(edges, "space")
    taps, gain = conv_taps.T, gain_matrix.T
    span = 2 if step_count % 2 == 0 else 1
    part, stats = frame_sums(taps, observed, frames, pooling)
    gain_part = gain_sums(observed, above, below, part, taps, pooling, gain)
    map_high, map_low, grams, first_gram = prepare(
        transition, update_map, quiet_root, observed_root, init_root
    )
    shifts = total(gain_part, "chan")
    gradient = tap_sums(observed, edges, above, below, stats, taps, rows)
    shifts = total(shifts, "space")
    flag_row = jnp.pad(observed.astype(F32)[None], ((0, 0), (0, shifts.shape[1] - step_count)))
    held = history(jnp.concatenate([shifts, flag_row], axis=0)[None], "tm")
    flags = held[:, step_count, :step_count].astype(jnp.int32).reshape(-1)
    if span == 2:
        span_high, span_low, span_gram = pair_maps(map_high, map_low, grams)
    else:
        span_high, span_low, span_gram = map_high, map_low, grams
    gradient = total(gradient, "space")
    gram = recursion(place, flags, step_count, span, span_high, span_low, span_gram, first_gram)
    root, filtered_means = factor(
        place, flags, step_count, span, gram,
        map_high, map_low, span_high, span_low, held, init_mean,
    )
    return (filtered_means, root[None], gradient.T[None])


def solution(mesh):
    return jax.shard_map(
        local,
        mesh=mesh,
        in_specs=(
            P(("groups", "tm"), "chan", "space", None),
            P("chan", None),
            P("space", None),
            P(None, ("space", "chan")),
            P(),
            P(),
            P(),
            P(),
            P("groups"),
            P("groups", None),
            P(("groups", "tm")),
        ),
        out_specs=(
            P(("groups", "tm"), None),
            P(("groups", "tm"), None, None),
            P(("groups", "tm"), "chan", None),
        ),
        check_vma=False,
    )
```

```python
import math

import jax
import jax.numpy as jnp
import numpy as np
from jax import lax
from jax.experimental import pallas as pl
from jax.experimental.pallas import tpu as pltpu
from jax.sharding import PartitionSpec as P


DILATION_STEP = 2
PANEL = 32
GROUP = 8
LANES = 128
F32 = jnp.float32
BF16 = jnp.bfloat16

precise = lax.Precision.HIGHEST
SMALL = pltpu.CompilerParams(vmem_limit_bytes=16 * 2**20)


def history(own, axis):
    count = lax.axis_size(axis)
    if count <= 4:
        held = [own]
        for lag in range(1, count):
            ring = [(i, (i + lag) % count) for i in range(count)]
            held.append(lax.ppermute(own, axis, ring))
        return jnp.concatenate(held, axis=0)
    held = own
    reach = 1
    while reach < count:
        pairs = [(i, i + reach) for i in range(count - reach)]
        held = jnp.concatenate([held, lax.ppermute(held, axis, pairs)], axis=0)
        reach *= 2
    return held


def on_chip(*arrays):
    return [pltpu.with_memory_space_constraint(array, pltpu.VMEM) for array in arrays]


def split(x):
    high = x.astype(BF16)
    return high, (x - high.astype(F32)).astype(BF16)


def contract(a, b, dims):
    return lax.dot_general(a, b, (dims, ((), ())), preferred_element_type=F32)


def three_pass(a, b, dims):
    return (
        contract(a[0], b[0], dims)
        + contract(a[0], b[1], dims)
        + contract(a[1], b[0], dims)
    )


def exact(a, b, dims):
    return lax.dot_general(
        a, b, (dims, ((), ())), precision=precise, preferred_element_type=F32
    )


NN = ((1,), (0,))
NT = ((1,), (1,))
TN = ((0,), (0,))


def prepare_kernel(
    transition, update_map, quiet_root, observed_root, init_root,
    map_high, map_low, grams, first_gram,
):
    for which, ref in enumerate((transition, update_map)):
        map_high[which], map_low[which] = split(ref[...])
    for which, ref in enumerate((quiet_root, observed_root)):
        pair = split(ref[...])
        grams[which] = three_pass(pair, pair, TN)
    pair = split(init_root[...])
    first_gram[...] = three_pass(pair, pair, TN)


def prepare(transition, update_map, quiet_root, observed_root, init_root):
    size = transition.shape[0]
    return pl.pallas_call(
        prepare_kernel,
        out_shape=(
            pltpu.VMEM((2, size, size), BF16),
            pltpu.VMEM((2, size, size), BF16),
            pltpu.VMEM((2, size, size), F32),
            pltpu.VMEM((size, size), F32),
        ),
        compiler_params=SMALL,
        name="prepare",
    )(*on_chip(transition, update_map, quiet_root, observed_root, init_root))


def pairs_kernel(map_high, map_low, grams, pair_high, pair_low, pair_gram):
    maps = [(map_high[which], map_low[which]) for which in range(2)]
    for later in range(2):
        for earlier in range(2):
            which = 2 * later + earlier
            joined = three_pass(maps[later], maps[earlier], NN)
            pair_high[which], pair_low[which] = split(joined)
            carried = three_pass(maps[later], split(grams[earlier]), NN)
            pair_gram[which] = three_pass(split(carried), maps[later], NT) + grams[later]


def pair_maps(map_high, map_low, grams):
    size = grams.shape[1]
    return pl.pallas_call(
        pairs_kernel,
        out_shape=(
            pltpu.VMEM((4, size, size), BF16),
            pltpu.VMEM((4, size, size), BF16),
            pltpu.VMEM((4, size, size), F32),
        ),
        compiler_params=SMALL,
        name="pair_maps",
    )(*on_chip(map_high, map_low, grams))


def upper_factor(gram, out, high, low, beside_work=()):
    size = gram.shape[0]
    halves = size // LANES
    tile = (GROUP, LANES)
    zero = jnp.zeros(tile, F32)
    sub = lax.broadcasted_iota(jnp.int32, tile, 0)
    lane = lax.broadcasted_iota(jnp.int32, tile, 1)
    count = PANEL // GROUP
    pending = list(beside_work)
    for top in range(0, size, PANEL):
        first = top // LANES
        start = first * LANES
        panel = gram[top : top + PANEL, start:]
        if top:
            left = (high[:top, top : top + PANEL], low[:top, top : top + PANEL])
            panel = panel - three_pass(left, (high[:top, start:], low[:top, start:]), TN)
        places = range(halves - first)
        part = [
            [
                panel[GROUP * i : GROUP * (i + 1), LANES * h : LANES * (h + 1)]
                for h in places
            ]
            for i in range(count)
        ]
        done = [[zero for _ in places] for _ in range(count)]
        for g in range(count):
            if pending:
                pending.pop(0)()
            base = top + GROUP * g
            here, at = base // LANES - first, base % LANES
            live = range(here, halves - first)
            column = {
                i: [
                    jnp.broadcast_to(part[i][here][:, at + j : at + j + 1], tile)
                    for j in range(GROUP)
                ]
                for i in range(g, count)
            }
            pivot = {
                (j, m): jnp.broadcast_to(column[g][m][j : j + 1, :], tile)
                for j in range(GROUP)
                for m in range(j, GROUP)
            }
            factor, scale = {}, []
            for j in range(GROUP):
                scale.append(lax.rsqrt(pivot[j, j]))
                for m in range(j + 1, GROUP):
                    factor[j, m] = pivot[j, m] * scale[j]
                for i in range(j + 1, GROUP):
                    for m in range(i, GROUP):
                        pivot[i, m] = pivot[i, m] - factor[j, i] * factor[j, m]
            rows = {}
            for h in live:
                rows[h] = []
                for j in range(GROUP):
                    value = jnp.broadcast_to(part[g][h][j : j + 1, :], tile)
                    for i in range(j):
                        value = value - factor[i, j] * rows[h][i]
                    rows[h].append(value * scale[j])
                value = rows[h][0]
                for j in range(1, GROUP):
                    value = jnp.where(sub == j, rows[h][j], value)
                if h == here:
                    value = jnp.where(lane - at >= sub, value, 0.0)
                done[g][h] = value
            for i in range(g + 1, count):
                left = []
                for j in range(GROUP):
                    value = column[i][j]
                    for m in range(j):
                        value = value - factor[m, j] * left[m]
                    left.append(value * scale[j])
                for h in live:
                    value = part[i][h]
                    for j in range(GROUP):
                        value = value - left[j] * rows[h][j]
                    part[i][h] = value
        for i in range(count):
            low_row = top + GROUP * i
            for h in range(halves):
                value = done[i][h - first] if h >= first else zero
                out[low_row : low_row + GROUP, LANES * h : LANES * (h + 1)] = value
        if top + PANEL < size:
            rows_high, rows_low = split(out[top : top + PANEL, :])
            high[top : top + PANEL, :] = rows_high
            low[top : top + PANEL, :] = rows_low
    for work in pending:
        work()


def recursion_kernel(steps, span, place, flags, span_high, span_low, span_gram, first_gram, gram):
    index = place[0]
    pieces = steps // span
    gram[...] = first_gram[...]

    def step(n, carry):
        at = (index - n // pieces) * steps + (n % pieces) * span
        which = flags[at]
        for later in range(1, span):
            which = which + flags[at + later] * 2**later
        map_pair = (span_high[which], span_low[which])
        old = split(gram[...])
        half = gram.shape[0] // 2
        new = []
        for at in (0, half):
            left = (map_pair[0][at : at + half], map_pair[1][at : at + half])
            carried = three_pass(left, old, NN)
            new.append(
                three_pass(split(carried), map_pair, NT) + span_gram[which, at : at + half]
            )
        for n_half, at in enumerate((0, half)):
            gram[at : at + half] = new[n_half]
        return carry

    lax.fori_loop(0, (index + 1) * pieces, step, 0)


def recursion(place, flags, steps, span, span_high, span_low, span_gram, first_gram):
    vmem = pl.BlockSpec(memory_space=pltpu.VMEM)
    smem = pl.BlockSpec(memory_space=pltpu.SMEM)

    def kernel(*refs):
        recursion_kernel(steps, span, *refs)

    return pl.pallas_call(
        kernel,
        out_shape=pltpu.VMEM(first_gram.shape, F32),
        in_specs=[smem, smem, vmem, vmem, vmem, vmem],
        out_specs=vmem,
        compiler_params=SMALL,
        name="recursion",
    )(place, flags, *on_chip(span_high, span_low, span_gram, first_gram))


def factor_kernel(
    steps, span, place, flags, gram, map_high, map_low, span_high, span_low, shifts, init_mean,
    out, mean_out, high, low, carried,
):
    index = place[0]
    size = gram.shape[0]
    blocks = shifts.shape[0]
    state = {"mean": jnp.broadcast_to(init_mean[...], (GROUP, size))}

    def first():
        rows = split(jnp.concatenate([shifts[block] for block in range(blocks)], axis=0))
        for which in range(2):
            carried[which] = three_pass(rows, (map_high[which], map_low[which]), NT)

    def one_step(block, t):
        at = block * steps + t
        flag = flags[at]
        mean = three_pass(split(state["mean"]), (map_high[flag], map_low[flag]), NT)
        return mean + shifts[block, t : t + 1, :]

    def work(block, t):
        def run():
            if block == 0:
                mean = one_step(block, t)
                mean_out[t : t + 1, :] = mean[0:1]
                if span == 1:
                    state["mean"] = mean
                    return
            if span == 1:
                mean = one_step(block, t)
            else:
                at = block * steps + t
                which = flags[at] + 2 * flags[at + 1]
                mean = three_pass(split(state["mean"]), (span_high[which], span_low[which]), NT)
                row = block * shifts.shape[1] + t
                mean = mean + carried[flags[at + 1], row : row + 1, :]
                mean = mean + shifts[block, t + 1 : t + 2, :]
                if block == 0:
                    mean_out[t + 1 : t + 2, :] = mean[0:1]
            state["mean"] = mean if block == 0 else jnp.where(block <= index, mean, state["mean"])

        return run

    jobs = [first] if span == 2 else []
    jobs += [work(block, t) for block in reversed(range(blocks)) for t in range(0, steps, span)]
    upper_factor(gram, out, high, low, jobs)


def factor(
    place, flags, steps, span, gram, map_high, map_low, span_high, span_low, shifts, init_mean
):
    size = gram.shape[0]
    vmem = pl.BlockSpec(memory_space=pltpu.VMEM)
    smem = pl.BlockSpec(memory_space=pltpu.SMEM)

    def kernel(*refs):
        factor_kernel(steps, span, *refs)

    return pl.pallas_call(
        kernel,
        out_shape=(
            jax.ShapeDtypeStruct((size, size), F32),
            jax.ShapeDtypeStruct((steps, size), F32),
        ),
        in_specs=[smem, smem] + [vmem] * 7,
        out_specs=(vmem, vmem),
        scratch_shapes=[
            pltpu.VMEM((size, size), BF16),
            pltpu.VMEM((size, size), BF16),
            pltpu.VMEM((2, shifts.shape[0] * shifts.shape[1], size), F32),
        ],
        compiler_params=SMALL,
        name="factor",
    )(
        place,
        flags,
        *on_chip(gram, map_high, map_low, span_high, span_low, shifts, init_mean[None]),
    )


LAGS = (0, DILATION_STEP, 2 * DILATION_STEP, -DILATION_STEP, -2 * DILATION_STEP)
TAPS = tuple((a, b) for a in (-1, 0, 1) for b in (-1, 0, 1))
EDGE = 2 * DILATION_STEP
KINDS = 8
EDGE_KINDS = 2
HALO_KINDS = 6


def moved(x, by, axis):
    if by == 0:
        return x
    length = x.shape[axis]
    shape = list(x.shape)
    shape[axis] = abs(by)
    zeros = jnp.zeros(shape, x.dtype)
    if by > 0:
        return jnp.concatenate(
            [lax.slice_in_dim(x, by, length, axis=axis), zeros], axis=axis
        )
    return jnp.concatenate(
        [zeros, lax.slice_in_dim(x, 0, length + by, axis=axis)], axis=axis
    )


def folded(x):
    total = x[:, :LANES]
    for at in range(LANES, x.shape[1], LANES):
        total = total + x[:, at : at + LANES]
    return total


def frames_kernel(unroll, taps, flags, frames, pooling, part, stats, pooled):
    steps, channels, rows, columns = frames.shape
    for k, (a, b) in enumerate(TAPS):
        pooled[k] = moved(
            moved(pooling[...], -DILATION_STEP * b, 1), -DILATION_STEP * a, 0
        )
    lane = lax.broadcasted_iota(jnp.int32, (rows, LANES), 1)
    row = lax.broadcasted_iota(jnp.int32, (rows, LANES), 0)
    masks = [lax.rem(lane, rows) - row == lag for lag in LAGS]
    right_masks = [(lane - row == lag) & (lane < rows) for lag in LAGS[:3]]
    column = lax.broadcasted_iota(jnp.int32, (rows, columns), 1)
    left_edge = (column < DILATION_STEP).astype(F32).astype(BF16)
    right_edge = (column >= columns - DILATION_STEP).astype(F32).astype(BF16)
    blank = jnp.zeros((rows, 2 * LANES - 5 * rows), F32)

    def channel(c):
        weights = taps[0, c] * pooled[0]
        for k in range(1, len(TAPS)):
            weights = weights + taps[k, c] * pooled[k]
        gram = jnp.zeros((rows, 5 * rows), F32)
        for t in range(steps):
            frame = frames[t, c]
            part[t, pl.ds(c, 1), :] = jnp.sum(
                folded(frame.astype(F32) * weights), axis=0, keepdims=True
            )
            partners = jnp.concatenate(
                [
                    frame,
                    moved(frame, DILATION_STEP, 1),
                    moved(frame, 2 * DILATION_STEP, 1),
                    frame * left_edge,
                    frame * right_edge,
                ],
                axis=0,
            )
            gram = gram + contract(frame * flags[t].astype(F32).astype(BF16), partners, NT)
        near = gram[:, :LANES]
        far = jnp.concatenate([gram[:, LANES:], blank], axis=1)
        sums = [jnp.sum(jnp.where(m, near, 0.0), axis=0, keepdims=True) for m in masks]
        sums += [jnp.sum(jnp.where(m, far, 0.0), axis=0, keepdims=True) for m in right_masks]
        stats[pl.ds(c, 1), :] = jnp.concatenate(sums, axis=1)

    def several(n, carry):
        for u in range(unroll):
            channel(n * unroll + u)
        return carry

    lax.fori_loop(0, channels // unroll, several, 0)


def frame_sums(taps, flags, frames, pooling):
    steps, channels, rows, columns = frames.shape
    vmem = pl.BlockSpec(memory_space=pltpu.VMEM)
    smem = pl.BlockSpec(memory_space=pltpu.SMEM)

    def kernel(*refs):
        frames_kernel(math.gcd(channels, 8), *refs)

    return pl.pallas_call(
        kernel,
        out_shape=(
            pltpu.VMEM((steps, channels, LANES), F32),
            pltpu.VMEM((channels, KINDS * LANES), F32),
        ),
        in_specs=[smem, smem, vmem, vmem],
        out_specs=(vmem, vmem),
        scratch_shapes=[pltpu.VMEM((len(TAPS), rows, columns), F32)],
        compiler_params=SMALL,
        name="frame_sums",
    )(taps, flags, *on_chip(frames, pooling))


def selection(rows):
    near = np.zeros((KINDS, LANES, len(TAPS), len(TAPS)), np.float32)
    edge = np.zeros((EDGE_KINDS, LANES, len(TAPS), len(TAPS)), np.float32)
    halo = np.zeros((2, HALO_KINDS, LANES, len(TAPS), len(TAPS)), np.float32)
    own = np.arange(rows)
    top, bottom = own[:DILATION_STEP], own[rows - DILATION_STEP :]
    for i, (a, b) in enumerate(TAPS):
        for j, (c, d) in enumerate(TAPS):
            down, across = c - a, d - b
            if (down, across) < (0, 0):
                down, across = -down, -across
            lag = abs(across)
            kind = down if across >= 0 else down + 2
            near[kind, lag * rows + own, i, j] += 1
            if down:
                if across == 0:
                    halo[down - 1, :2, :, i, j] += 1
                else:
                    halo[down - 1, 1 + lag + (2 if across < 0 else 0), :, i, j] += 1
            if b == d == 1:
                near[down, 3 * rows + own, i, j] -= 1
                if down:
                    halo[down - 1, 0, :DILATION_STEP, i, j] -= 1
            if b == d == -1:
                near[5 + down, own, i, j] -= 1
                if down:
                    halo[down - 1, 1, LANES - DILATION_STEP :, i, j] -= 1
            if a == c != 0:
                lost = top if a == 1 else bottom
                edge[0, lag * rows + lost, i, j] -= 1
                if b == d == 1:
                    edge[0, 3 * rows + lost, i, j] += 1
                if b == d == -1:
                    edge[1, lost, i, j] += 1
    pairs = len(TAPS) ** 2
    table = np.concatenate([m.reshape(-1, pairs) for m in (near, edge, halo)], axis=0)
    return np.pad(table, ((0, 0), (0, LANES - pairs)))


def beside_tile():
    place, count = lax.axis_index("space"), lax.axis_size("space")
    has_above = jnp.where(place > 0, 1.0, 0.0).astype(F32)
    has_below = jnp.where(place < count - 1, 1.0, 0.0).astype(F32)
    return has_above, has_below


def spread():
    shape = (len(TAPS), LANES)
    source = lax.broadcasted_iota(jnp.int32, shape, 1)
    return source, lax.broadcasted_iota(jnp.int32, shape, 0)


def gain_kernel(flags, above, below, part, taps, pooling, gain, gain_part):
    steps, _, channels, columns = above.shape
    rows = pooling.shape[0]
    has_above, has_below = beside_tile()
    source, tap = spread()
    tap_columns = exact(taps[...], (source == tap).astype(F32), TN)
    halo_weights = []
    for a, start, has in ((-1, 0, has_above), (1, rows - DILATION_STEP, has_below)):
        for r in range(DILATION_STEP):
            value = jnp.zeros((channels, columns), F32)
            for b in (-1, 0, 1):
                k = TAPS.index((a, b))
                shifted = moved(pooling[start + r : start + r + 1, :], -DILATION_STEP * b, 1)
                value = value + tap_columns[:, k : k + 1] * shifted
            halo_weights.append(value * has)
    row_sums = []
    for t in range(steps):
        total = jnp.zeros((channels, columns), F32)
        for r in range(DILATION_STEP):
            total = total + above[t, r].astype(F32) * halo_weights[r]
            total = total + below[t, r].astype(F32) * halo_weights[DILATION_STEP + r]
        row_sums.append(part[t] + folded(total))
    ones = jnp.ones((GROUP, LANES), BF16)
    high, low = split(jnp.concatenate(row_sums, axis=0))
    tile_sums = contract(ones, high, NT) + contract(ones, low, NT)
    shape = (GROUP, steps * channels)
    owner = lax.broadcasted_iota(jnp.int32, shape, 1) // channels
    step = lax.broadcasted_iota(jnp.int32, shape, 0)
    seen = jnp.zeros(shape, F32)
    for t in range(steps):
        seen = jnp.where((owner == t) & (step == t), flags[t].astype(F32), seen)
    gains = jnp.concatenate([gain[...]] * steps, axis=0)
    product = three_pass(split(tile_sums * seen), split(gains), NN)
    gain_part[...] = product[:steps]


def gain_sums(flags, above, below, part, taps, pooling, gain):
    vmem = pl.BlockSpec(memory_space=pltpu.VMEM)
    smem = pl.BlockSpec(memory_space=pltpu.SMEM)
    return pl.pallas_call(
        gain_kernel,
        out_shape=jax.ShapeDtypeStruct((above.shape[0], gain.shape[1]), F32),
        in_specs=[smem] + [vmem] * 6,
        out_specs=vmem,
        compiler_params=SMALL,
        name="gain_sums",
    )(flags, *on_chip(above, below, part, taps, pooling, gain))


def gradient_kernel(
    scale, rows, flags, edges, above, below, stats, taps, table, gradient, values
):
    steps, _, channels, columns = edges.shape
    has_above, has_below = beside_tile()
    sums = [[None] * 5 for _ in range(2)]
    for t in range(steps):
        flag = flags[t].astype(F32)
        for r in range(DILATION_STEP):
            near_top = edges[t, DILATION_STEP + r].astype(F32)
            far_bottom = edges[t, 2 * DILATION_STEP + r].astype(F32)
            near_bottom = edges[t, 3 * DILATION_STEP + r].astype(F32)
            high = above[t, r].astype(F32) * (flag * has_above)
            low = below[t, r].astype(F32) * (flag * has_below)
            for n in range(-2, 3):
                shifted_low = moved(low, DILATION_STEP * n, 1)
                shifted_high = moved(high, -DILATION_STEP * n, 1)
                one = near_bottom * shifted_low
                two = far_bottom * shifted_low + near_top * shifted_high
                for which, value in ((0, one), (1, two)):
                    old = sums[which][n]
                    sums[which][n] = value if old is None else old + value
    values[:, : KINDS * LANES] = stats[...]
    lane = lax.rem(lax.broadcasted_iota(jnp.int32, (channels, LANES), 1), rows)
    outside = jnp.where(lane < DILATION_STEP, 1.0 - has_above, 0.0)
    outside = jnp.where(lane >= rows - DILATION_STEP, 1.0 - has_below, outside)
    at = KINDS * LANES
    for kind in (0, 5):
        values[:, at : at + LANES] = stats[:, kind * LANES : (kind + 1) * LANES] * outside
        at += LANES
    for which in range(2):
        centre = sums[which][0]
        pieces = [centre[:, :LANES], centre[:, columns - LANES :]]
        pieces += [folded(sums[which][n]) for n in (1, 2, -1, -2)]
        for inner in range(LANES, columns - LANES, LANES):
            middle = jnp.sum(centre[:, inner : inner + LANES], axis=1, keepdims=True)
            pieces[0] = pieces[0] + jnp.where(lane_of(channels) == LANES // 2, middle, 0.0)
        for piece in pieces:
            values[:, at : at + LANES] = piece
            at += LANES
    high, low = split(values[...])
    pairs = contract(high, table[...], NN) + contract(low, table[...], NN)
    source, tap = spread()
    weights = exact(taps[...], (source // len(TAPS) == tap).astype(F32), TN)
    gathered = (source % len(TAPS) == tap).astype(F32)
    gradient[...] = exact(gathered, pairs * weights, NT) * scale


def lane_of(channels):
    return lax.broadcasted_iota(jnp.int32, (channels, LANES), 1)


def tap_sums(flags, edges, above, below, stats, taps, rows):
    _, _, channels, columns = edges.shape
    scale = 1.0 / (rows * lax.axis_size("space") * columns)
    table = jnp.asarray(selection(rows), BF16)
    vmem = pl.BlockSpec(memory_space=pltpu.VMEM)
    smem = pl.BlockSpec(memory_space=pltpu.SMEM)

    def kernel(*refs):
        gradient_kernel(scale, rows, *refs)

    return pl.pallas_call(
        kernel,
        out_shape=jax.ShapeDtypeStruct((len(TAPS), channels), F32),
        in_specs=[smem] + [vmem] * 6,
        out_specs=vmem,
        scratch_shapes=[pltpu.VMEM((channels, table.shape[0]), F32)],
        compiler_params=SMALL,
        name="tap_sums",
    )(flags, *on_chip(edges, above, below, stats, taps, table))


def beside(edges, axis):
    count = lax.axis_size(axis)
    top = edges[:, :DILATION_STEP]
    bottom = edges[:, -DILATION_STEP:]
    if count == 2:
        sent = jnp.where(lax.axis_index(axis) == 0, bottom, top)
        got = lax.ppermute(sent, axis, [(0, 1), (1, 0)])
        return got, got
    forward = [(i, (i + 1) % count) for i in range(count)]
    backward = [(target, source) for source, target in forward]
    return lax.ppermute(bottom, axis, forward), lax.ppermute(top, axis, backward)


def total(value, axis):
    if lax.axis_size(axis) == 2:
        return value + lax.ppermute(value, axis, [(0, 1), (1, 0)])
    return lax.psum(value, axis)


def local(
    frames,
    conv_taps,
    pooling,
    gain_matrix,
    transition,
    update_map,
    quiet_root,
    observed_root,
    init_mean,
    init_root,
    observed,
):
    step_count, _, rows, _ = frames.shape
    place = lax.axis_index("tm").astype(jnp.int32)[None]
    edges = jnp.concatenate([frames[:, :, :EDGE], frames[:, :, rows - EDGE :]], axis=2)
    edges = edges.transpose(0, 2, 1, 3)
    above, below = beside(edges, "space")
    taps, gain = conv_taps.T, gain_matrix.T
    span = 2 if step_count % 2 == 0 else 1
    part, stats = frame_sums(taps, observed, frames, pooling)
    gain_part = gain_sums(observed, above, below, part, taps, pooling, gain)
    map_high, map_low, grams, first_gram = prepare(
        transition, update_map, quiet_root, observed_root, init_root
    )
    shifts = total(gain_part, "chan")
    gradient = tap_sums(observed, edges, above, below, stats, taps, rows)
    shifts = total(shifts, "space")
    flag_row = jnp.pad(observed.astype(F32)[None], ((0, 0), (0, shifts.shape[1] - step_count)))
    held = history(jnp.concatenate([shifts, flag_row], axis=0)[None], "tm")
    flags = held[:, step_count, :step_count].astype(jnp.int32).reshape(-1)
    if span == 2:
        span_high, span_low, span_gram = pair_maps(map_high, map_low, grams)
    else:
        span_high, span_low, span_gram = map_high, map_low, grams
    gradient = total(gradient, "space")
    gram = recursion(place, flags, step_count, span, span_high, span_low, span_gram, first_gram)
    root, filtered_means = factor(
        place, flags, step_count, span, gram,
        map_high, map_low, span_high, span_low, held, init_mean,
    )
    return (filtered_means, root[None], gradient.T[None])


def solution(mesh):
    return jax.shard_map(
        local,
        mesh=mesh,
        in_specs=(
            P(("groups", "tm"), "chan", "space", None),
            P("chan", None),
            P("space", None),
            P(None, ("space", "chan")),
            P(),
            P(),
            P(),
            P(),
            P("groups"),
            P("groups", None),
            P(("groups", "tm")),
        ),
        out_specs=(
            P(("groups", "tm"), None),
            P(("groups", "tm"), None, None),
            P(("groups", "tm"), "chan", None),
        ),
        check_vma=False,
    )
```

```python
import math

import jax
import jax.numpy as jnp
import numpy as np
from jax import lax
from jax.experimental import pallas as pl
from jax.experimental.pallas import tpu as pltpu
from jax.sharding import PartitionSpec as P


DILATION_STEP = 2
PANEL = 32
GROUP = 8
LANES = 128
F32 = jnp.float32
BF16 = jnp.bfloat16

precise = lax.Precision.HIGHEST
SMALL = pltpu.CompilerParams(vmem_limit_bytes=16 * 2**20)


def paired(count):
    return count & (count - 1) == 0


def slot_of(block, place, count):
    return block ^ place if paired(count) else block


def join_kernel(a, b, out):
    length = a.shape[0]
    out[:length] = a[...]
    out[length:] = b[...]


def joined(a, b):
    return pl.pallas_call(
        join_kernel,
        out_shape=jax.ShapeDtypeStruct((2 * a.shape[0],) + a.shape[1:], a.dtype),
        compiler_params=SMALL,
        name="joined",
    )(*on_chip(a, b))


def add_kernel(a, b, out):
    out[...] = a[...] + b[...]


def added(a, b):
    return pl.pallas_call(
        add_kernel,
        out_shape=jax.ShapeDtypeStruct(a.shape, a.dtype),
        compiler_params=SMALL,
        name="added",
    )(*on_chip(a, b))


def history(own, axis):
    count = lax.axis_size(axis)
    if not paired(count):
        return [lax.all_gather(own[0], axis)]
    pieces = [own]
    reach = 1
    while reach < count:
        sent = pieces[0]
        for piece in pieces[1:]:
            sent = joined(sent, piece)
        pieces.append(lax.ppermute(sent, axis, [(i, i ^ reach) for i in range(count)]))
        reach *= 2
    return pieces


def on_chip(*arrays):
    return [pltpu.with_memory_space_constraint(array, pltpu.VMEM) for array in arrays]


def split(x):
    high = x.astype(BF16)
    return high, (x - high.astype(F32)).astype(BF16)


def contract(a, b, dims):
    return lax.dot_general(a, b, (dims, ((), ())), preferred_element_type=F32)


def three_pass(a, b, dims):
    return (
        contract(a[0], b[0], dims)
        + contract(a[0], b[1], dims)
        + contract(a[1], b[0], dims)
    )


def exact(a, b, dims):
    return lax.dot_general(
        a, b, (dims, ((), ())), precision=precise, preferred_element_type=F32
    )


NN = ((1,), (0,))
NT = ((1,), (1,))
TN = ((0,), (0,))


def prepare_kernel(
    span, transition, update_map, quiet_root, observed_root, init_root,
    map_high, map_low, span_high, span_low, span_gram, first_gram,
):
    maps = [split(transition[...]), split(update_map[...])]
    for which, (high, low) in enumerate(maps):
        map_high[which] = high
        map_low[which] = low
    grams = []
    for ref in (quiet_root, observed_root):
        pair = split(ref[...])
        grams.append(three_pass(pair, pair, TN))
    pair = split(init_root[...])
    first_gram[...] = three_pass(pair, pair, TN)
    if span == 1:
        for which, (high, low) in enumerate(maps):
            span_high[which] = high
            span_low[which] = low
            span_gram[which] = grams[which]
        return
    for later in range(2):
        for earlier in range(2):
            which = 2 * later + earlier
            span_high[which], span_low[which] = split(
                three_pass(maps[later], maps[earlier], NN)
            )
            carried = three_pass(maps[later], split(grams[earlier]), NN)
            span_gram[which] = three_pass(split(carried), maps[later], NT) + grams[later]


def prepare(span, transition, update_map, quiet_root, observed_root, init_root):
    size = transition.shape[0]
    many = 2**span

    def kernel(*refs):
        prepare_kernel(span, *refs)

    return pl.pallas_call(
        kernel,
        out_shape=(
            pltpu.VMEM((2, size, size), BF16),
            pltpu.VMEM((2, size, size), BF16),
            pltpu.VMEM((many, size, size), BF16),
            pltpu.VMEM((many, size, size), BF16),
            pltpu.VMEM((many, size, size), F32),
            pltpu.VMEM((size, size), F32),
        ),
        compiler_params=SMALL,
        name="prepare",
    )(*on_chip(transition, update_map, quiet_root, observed_root, init_root))


def upper_factor(gram, out, high, low, begin, end, beside_work=()):
    size = gram.shape[0]
    halves = size // LANES
    tile = (GROUP, LANES)
    zero = jnp.zeros(tile, F32)
    sub = lax.broadcasted_iota(jnp.int32, tile, 0)
    lane = lax.broadcasted_iota(jnp.int32, tile, 1)
    count = PANEL // GROUP
    pending = list(beside_work)
    for top in range(begin, end, PANEL):
        first = top // LANES
        start = first * LANES
        panel = gram[top : top + PANEL, start:]
        if top:
            left = (high[:top, top : top + PANEL], low[:top, top : top + PANEL])
            panel = panel - three_pass(left, (high[:top, start:], low[:top, start:]), TN)
        places = range(halves - first)
        part = [
            [
                panel[GROUP * i : GROUP * (i + 1), LANES * h : LANES * (h + 1)]
                for h in places
            ]
            for i in range(count)
        ]
        done = [[zero for _ in places] for _ in range(count)]
        for g in range(count):
            if pending:
                pending.pop(0)()
            base = top + GROUP * g
            here, at = base // LANES - first, base % LANES
            live = range(here, halves - first)
            column = {
                i: [
                    jnp.broadcast_to(part[i][here][:, at + j : at + j + 1], tile)
                    for j in range(GROUP)
                ]
                for i in range(g, count)
            }
            pivot = {
                (j, m): jnp.broadcast_to(column[g][m][j : j + 1, :], tile)
                for j in range(GROUP)
                for m in range(j, GROUP)
            }
            factor, scale = {}, []
            for j in range(GROUP):
                scale.append(lax.rsqrt(pivot[j, j]))
                for m in range(j + 1, GROUP):
                    factor[j, m] = pivot[j, m] * scale[j]
                for i in range(j + 1, GROUP):
                    for m in range(i, GROUP):
                        pivot[i, m] = pivot[i, m] - factor[j, i] * factor[j, m]
            rows = {}
            for h in live:
                rows[h] = []
                for j in range(GROUP):
                    value = jnp.broadcast_to(part[g][h][j : j + 1, :], tile)
                    for i in range(j):
                        value = value - factor[i, j] * rows[h][i]
                    rows[h].append(value * scale[j])
                value = rows[h][0]
                for j in range(1, GROUP):
                    value = jnp.where(sub == j, rows[h][j], value)
                if h == here:
                    value = jnp.where(lane - at >= sub, value, 0.0)
                done[g][h] = value
            for i in range(g + 1, count):
                left = []
                for j in range(GROUP):
                    value = column[i][j]
                    for m in range(j):
                        value = value - factor[m, j] * left[m]
                    left.append(value * scale[j])
                for h in live:
                    value = part[i][h]
                    for j in range(GROUP):
                        value = value - left[j] * rows[h][j]
                    part[i][h] = value
        for i in range(count):
            low_row = top + GROUP * i
            for h in range(halves):
                value = done[i][h - first] if h >= first else zero
                out[low_row : low_row + GROUP, LANES * h : LANES * (h + 1)] = value
        if top + PANEL < size:
            rows_high, rows_low = split(out[top : top + PANEL, :])
            high[top : top + PANEL, :] = rows_high
            low[top : top + PANEL, :] = rows_low
    for work in pending:
        work()


def flag_reader(pieces, table):
    slot = 0
    for piece in pieces:
        for row in range(piece.shape[0]):
            for t in range(piece.shape[1]):
                table[slot + row, t] = piece[row, t]
        slot += piece.shape[0]
    return lambda slot, t: table[slot, t]


def recursion_kernel(
    steps, span, pieces, place, *refs
):
    flag_at = flag_reader(refs[:pieces], refs[-1])
    span_high, span_low, span_gram, first_gram, gram, _ = refs[pieces:]
    count = refs[-1].shape[0]
    index = place[0]
    parts = steps // span
    gram[...] = first_gram[...]

    def step(n, carry):
        slot = slot_of(n // parts, index, count)
        t = (n % parts) * span
        which = flag_at(slot, t)
        for later in range(1, span):
            which = which + flag_at(slot, t + later) * 2**later
        map_pair = (span_high[which], span_low[which])
        old = split(gram[...])
        half = gram.shape[0] // 2
        new = []
        for at in (0, half):
            left = (map_pair[0][at : at + half], map_pair[1][at : at + half])
            carried = three_pass(left, old, NN)
            new.append(
                three_pass(split(carried), map_pair, NT) + span_gram[which, at : at + half]
            )
        for n_half, at in enumerate((0, half)):
            gram[at : at + half] = new[n_half]
        return carry

    lax.fori_loop(0, (index + 1) * parts, step, 0)


def recursion(place, flags, steps, span, span_high, span_low, span_gram, first_gram):
    vmem = pl.BlockSpec(memory_space=pltpu.VMEM)
    smem = pl.BlockSpec(memory_space=pltpu.SMEM)

    def kernel(*refs):
        recursion_kernel(steps, span, len(flags), *refs)

    count = sum(piece.shape[0] for piece in flags)
    return pl.pallas_call(
        kernel,
        out_shape=pltpu.VMEM(first_gram.shape, F32),
        in_specs=[smem] * (1 + len(flags)) + [vmem] * 4,
        out_specs=vmem,
        scratch_shapes=[pltpu.SMEM((count, steps), jnp.int32)],
        compiler_params=SMALL,
        name="recursion",
    )(place, *flags, *on_chip(span_high, span_low, span_gram, first_gram))


def factor_top_kernel(gram, out, high, low):
    upper_factor(gram, out, high, low, 0, out.shape[0])


def factor_top(gram):
    size = gram.shape[0]
    rows = size // (2 * PANEL) * PANEL
    return pl.pallas_call(
        factor_top_kernel,
        out_shape=(
            pltpu.VMEM((rows, size), F32),
            pltpu.VMEM((rows, size), BF16),
            pltpu.VMEM((rows, size), BF16),
        ),
        compiler_params=SMALL,
        name="factor_top",
    )(*on_chip(gram))


def factor_kernel(
    steps, span, flag_pieces, shift_pieces, place, *refs
):
    flag_at = flag_reader(refs[:flag_pieces], refs[-1])
    gram, top, top_high, top_low, map_high, map_low = refs[flag_pieces : flag_pieces + 6]
    span_high, span_low, init_mean, gradient, gradient_beside = refs[
        flag_pieces + 6 : flag_pieces + 11
    ]
    received = refs[flag_pieces + 11 : flag_pieces + 11 + shift_pieces]
    out, mean_out, gradient_out, high, low, carried, shifts, _ = refs[
        flag_pieces + 11 + shift_pieces :
    ]
    index = place[0]
    size = gram.shape[0]
    count = shifts.shape[0]
    slot = 0
    for piece in received:
        shifts[slot : slot + piece.shape[0]] = piece[...]
        slot += piece.shape[0]
    begin = top.shape[0]
    gradient_out[:, 0, :] = gradient[...] + gradient_beside[...]
    out[:begin] = top[...]
    high[:begin] = top_high[...]
    low[:begin] = top_low[...]
    state = {"mean": jnp.broadcast_to(init_mean[...], (GROUP, size))}

    def first():
        rows = split(jnp.concatenate([shifts[slot] for slot in range(count)], axis=0))
        for which in range(2):
            values = three_pass(rows, (map_high[which], map_low[which]), NT)
            for slot in range(count):
                carried[which, slot] = values[slot * steps : (slot + 1) * steps]

    def work(block, t):
        own = block == count
        slot = slot_of(index, index, count) if own else slot_of(block, index, count)

        def one_step():
            flag = flag_at(slot, t)
            mean = three_pass(split(state["mean"]), (map_high[flag], map_low[flag]), NT)
            return mean + shifts[slot, t : t + 1, :]

        def run():
            if span == 1:
                mean = one_step()
            else:
                if own:
                    mean_out[t : t + 1, :] = one_step()[0:1]
                first_flag, last_flag = flag_at(slot, t), flag_at(slot, t + 1)
                which = first_flag + 2 * last_flag
                mean = three_pass(split(state["mean"]), (span_high[which], span_low[which]), NT)
                mean = mean + carried[last_flag, slot, t : t + 1, :]
                mean = mean + shifts[slot, t + 1 : t + 2, :]
            if own:
                mean_out[t + span - 1 : t + span, :] = mean[0:1]
            else:
                mean = jnp.where(block < index, mean, state["mean"])
            state["mean"] = mean

        return run

    jobs = [first] if span == 2 else []
    blocks = list(range(count - 1)) + [count]
    jobs += [work(block, t) for block in blocks for t in range(0, steps, span)]
    upper_factor(gram, out, high, low, begin, size, jobs)


def factor(
    place, flags, steps, span, gram, tops, map_high, map_low, span_high, span_low, shifts,
    init_mean, gradient, gradient_beside,
):
    size = gram.shape[0]
    taps, channels = gradient.shape
    count = sum(piece.shape[0] for piece in flags)
    vmem = pl.BlockSpec(memory_space=pltpu.VMEM)
    smem = pl.BlockSpec(memory_space=pltpu.SMEM)

    def kernel(*refs):
        factor_kernel(steps, span, len(flags), len(shifts), *refs)

    return pl.pallas_call(
        kernel,
        out_shape=(
            jax.ShapeDtypeStruct((size, size), F32),
            jax.ShapeDtypeStruct((steps, size), F32),
            jax.ShapeDtypeStruct((taps, 1, channels), F32),
        ),
        in_specs=[smem] * (1 + len(flags)) + [vmem] * (11 + len(shifts)),
        out_specs=(vmem, vmem, vmem),
        scratch_shapes=[
            pltpu.VMEM((size, size), BF16),
            pltpu.VMEM((size, size), BF16),
            pltpu.VMEM((2, count, steps, size), F32),
            pltpu.VMEM((count, steps, size), F32),
            pltpu.SMEM((count, steps), jnp.int32),
        ],
        compiler_params=SMALL,
        name="factor",
    )(
        place,
        *flags,
        *on_chip(
            gram, *tops, map_high, map_low, span_high, span_low, init_mean[None],
            gradient, gradient_beside, *shifts,
        ),
    )


LAGS = (0, DILATION_STEP, 2 * DILATION_STEP, -DILATION_STEP, -2 * DILATION_STEP)
TAPS = tuple((a, b) for a in (-1, 0, 1) for b in (-1, 0, 1))
EDGE = 2 * DILATION_STEP
KINDS = 8
EDGE_KINDS = 2
HALO_KINDS = 7


def moved(x, by, axis):
    if by == 0:
        return x
    length = x.shape[axis]
    shape = list(x.shape)
    shape[axis] = abs(by)
    zeros = jnp.zeros(shape, x.dtype)
    if by > 0:
        return jnp.concatenate(
            [lax.slice_in_dim(x, by, length, axis=axis), zeros], axis=axis
        )
    return jnp.concatenate(
        [zeros, lax.slice_in_dim(x, 0, length + by, axis=axis)], axis=axis
    )


def folded(x):
    total = x[:, :LANES]
    for at in range(LANES, x.shape[1], LANES):
        total = total + x[:, at : at + LANES]
    return total


def frames_kernel(
    unroll, taps, flags, source, pooling, part, stats, pooled, frames, arrived
):
    steps, channels, rows, columns = frames.shape
    copies = []
    for n in range(channels // unroll):
        piece = (slice(None), pl.ds(n * unroll, unroll))
        copies.append(
            pltpu.make_async_copy(source.at[piece], frames.at[piece], arrived.at[n])
        )
        copies[-1].start()
    for k, (a, b) in enumerate(TAPS):
        pooled[k] = moved(
            moved(pooling[...], -DILATION_STEP * b, 1), -DILATION_STEP * a, 0
        )
    lane = lax.broadcasted_iota(jnp.int32, (rows, LANES), 1)
    row = lax.broadcasted_iota(jnp.int32, (rows, LANES), 0)
    masks = [lax.rem(lane, rows) - row == lag for lag in LAGS]
    left_edge = (lane < DILATION_STEP).astype(F32).astype(BF16)
    right_edge = (lane >= LANES - DILATION_STEP).astype(F32).astype(BF16)
    left_half = (lane < LANES // 2).astype(F32).astype(BF16)
    right_half = (lane >= LANES // 2).astype(F32).astype(BF16)
    middle = LANES // 2 - DILATION_STEP
    blank = jnp.zeros((LANES - 3 * rows, columns), BF16)
    edge_blank = jnp.zeros((LANES - 2 * rows, LANES), BF16)

    def channel(c):
        weights = taps[0, c] * pooled[0]
        for k in range(1, len(TAPS)):
            weights = weights + taps[k, c] * pooled[k]
        gram = jnp.zeros((rows, LANES), F32)
        borders = jnp.zeros((rows, LANES), BF16)
        for t in range(steps):
            frame = frames[t, c]
            part[t, pl.ds(c, 1), :] = jnp.sum(
                folded(frame.astype(F32) * weights), axis=0, keepdims=True
            )
            partners = jnp.concatenate(
                [
                    frame,
                    moved(frame, DILATION_STEP, 1),
                    moved(frame, 2 * DILATION_STEP, 1),
                    blank,
                ],
                axis=0,
            )
            seen = frame * flags[t].astype(F32).astype(BF16)
            gram = gram + contract(seen, partners, NT)
            at = DILATION_STEP * t
            borders = borders + moved(seen[:, :LANES] * left_edge, -at, 1)
            borders = borders + moved(seen[:, columns - LANES :] * right_edge, middle - at, 1)
        edge = contract(
            borders,
            jnp.concatenate([borders * left_half, borders * right_half, edge_blank], axis=0),
            NT,
        )
        sums = [jnp.sum(jnp.where(m, gram, 0.0), axis=0, keepdims=True) for m in masks]
        sums += [jnp.sum(jnp.where(m, edge, 0.0), axis=0, keepdims=True) for m in masks[:3]]
        stats[pl.ds(c, 1), :] = jnp.concatenate(sums, axis=1)

    def several(n, carry):
        piece = (slice(None), pl.ds(n * unroll, unroll))
        pltpu.make_async_copy(source.at[piece], frames.at[piece], arrived.at[n]).wait()
        for u in range(unroll):
            channel(n * unroll + u)
        return carry

    lax.fori_loop(0, channels // unroll, several, 0)


def frame_sums(taps, flags, frames, pooling):
    steps, channels, rows, columns = frames.shape
    vmem = pl.BlockSpec(memory_space=pltpu.VMEM)
    smem = pl.BlockSpec(memory_space=pltpu.SMEM)

    unroll = math.gcd(channels, 8)

    def kernel(*refs):
        frames_kernel(unroll, *refs)

    return pl.pallas_call(
        kernel,
        out_shape=(
            pltpu.VMEM((steps, channels, LANES), F32),
            pltpu.VMEM((channels, KINDS * LANES), F32),
        ),
        in_specs=[smem, smem, pl.BlockSpec(memory_space=pltpu.HBM), vmem],
        out_specs=(vmem, vmem),
        scratch_shapes=[
            pltpu.VMEM((len(TAPS), rows, columns), F32),
            pltpu.VMEM(frames.shape, frames.dtype),
            pltpu.SemaphoreType.DMA((channels // unroll,)),
        ],
        compiler_params=SMALL,
        name="frame_sums",
    )(
        taps, flags, pltpu.with_memory_space_constraint(frames, pltpu.HBM), *on_chip(pooling)
    )


def selection(rows):
    near = np.zeros((KINDS, LANES, len(TAPS), len(TAPS)), np.float32)
    edge = np.zeros((EDGE_KINDS, LANES, len(TAPS), len(TAPS)), np.float32)
    halo = np.zeros((2, HALO_KINDS, len(TAPS), len(TAPS)), np.float32)
    own = np.arange(rows)
    top, bottom = own[:DILATION_STEP], own[rows - DILATION_STEP :]
    for i, (a, b) in enumerate(TAPS):
        for j, (c, d) in enumerate(TAPS):
            down, across = c - a, d - b
            if (down, across) < (0, 0):
                down, across = -down, -across
            lag = abs(across)
            kind = down if across >= 0 else down + 2
            near[kind, lag * rows + own, i, j] += 1
            if down:
                halo[down - 1, across + 2, i, j] += 1
            for side, group in ((1, 0), (-1, 1)):
                if b == d == side:
                    near[5 + down, group * rows + own, i, j] -= 1
                    if down:
                        halo[down - 1, 5 + group, i, j] -= 1
            if a == c != 0:
                lost = top if a == 1 else bottom
                edge[0, lag * rows + lost, i, j] -= 1
                for side, group in ((1, 0), (-1, 1)):
                    if b == d == side:
                        edge[1, group * rows + lost, i, j] += 1
    pairs = len(TAPS) ** 2
    table = np.concatenate([m.reshape(-1, pairs) for m in (near, edge)], axis=0)
    halo = np.pad(halo.reshape(-1, pairs), ((0, -2 * HALO_KINDS % GROUP), (0, 0)))
    return [np.pad(m, ((0, 0), (0, LANES - pairs))) for m in (table, halo)]


def beside_tile():
    place, count = lax.axis_index("space"), lax.axis_size("space")
    has_above = jnp.where(place > 0, 1.0, 0.0).astype(F32)
    has_below = jnp.where(place < count - 1, 1.0, 0.0).astype(F32)
    return has_above, has_below


def spread():
    shape = (len(TAPS), LANES)
    source = lax.broadcasted_iota(jnp.int32, shape, 1)
    return source, lax.broadcasted_iota(jnp.int32, shape, 0)


def gain_kernel(flags, above, below, part, taps, pooling, gain, gain_part):
    steps, _, channels, columns = above.shape
    rows = pooling.shape[0]
    has_above, has_below = beside_tile()
    source, tap = spread()
    tap_columns = exact(taps[...], (source == tap).astype(F32), TN)
    halo_weights = []
    for a, start, has in ((-1, 0, has_above), (1, rows - DILATION_STEP, has_below)):
        for r in range(DILATION_STEP):
            value = jnp.zeros((channels, columns), F32)
            for b in (-1, 0, 1):
                k = TAPS.index((a, b))
                shifted = moved(pooling[start + r : start + r + 1, :], -DILATION_STEP * b, 1)
                value = value + tap_columns[:, k : k + 1] * shifted
            halo_weights.append(value * has)
    row_sums = []
    for t in range(steps):
        total = jnp.zeros((channels, columns), F32)
        for r in range(DILATION_STEP):
            total = total + above[t, r].astype(F32) * halo_weights[r]
            total = total + below[t, r].astype(F32) * halo_weights[DILATION_STEP + r]
        row_sums.append(part[t] + folded(total))
    ones = jnp.ones((GROUP, LANES), BF16)
    high, low = split(jnp.concatenate(row_sums, axis=0))
    tile_sums = contract(ones, high, NT) + contract(ones, low, NT)
    shape = (GROUP, steps * channels)
    owner = lax.broadcasted_iota(jnp.int32, shape, 1) // channels
    step = lax.broadcasted_iota(jnp.int32, shape, 0)
    seen = jnp.zeros(shape, F32)
    for t in range(steps):
        seen = jnp.where((owner == t) & (step == t), flags[t].astype(F32), seen)
    gains = jnp.concatenate([gain[...]] * steps, axis=0)
    product = three_pass(split(tile_sums * seen), split(gains), NN)
    gain_part[...] = product[:steps]


def gain_sums(flags, above, below, part, taps, pooling, gain):
    vmem = pl.BlockSpec(memory_space=pltpu.VMEM)
    smem = pl.BlockSpec(memory_space=pltpu.SMEM)
    return pl.pallas_call(
        gain_kernel,
        out_shape=jax.ShapeDtypeStruct((above.shape[0], gain.shape[1]), F32),
        in_specs=[smem] + [vmem] * 6,
        out_specs=vmem,
        compiler_params=SMALL,
        name="gain_sums",
    )(flags, *on_chip(above, below, part, taps, pooling, gain))


def gradient_kernel(
    scale, rows, flags, tops, bottoms, above, below, stats, taps, table, halo_table,
    gradient, values,
):
    steps, _, channels, columns = tops.shape
    has_above, has_below = beside_tile()
    sums = [[None] * 5 for _ in range(2)]
    for t in range(steps):
        flag = flags[t].astype(F32)
        for r in range(DILATION_STEP):
            near_top = tops[t, DILATION_STEP + r].astype(F32)
            far_bottom = bottoms[t, r].astype(F32)
            near_bottom = bottoms[t, DILATION_STEP + r].astype(F32)
            high = above[t, r].astype(F32) * (flag * has_above)
            low = below[t, r].astype(F32) * (flag * has_below)
            for n in range(-2, 3):
                shifted_low = moved(low, DILATION_STEP * n, 1)
                shifted_high = moved(high, -DILATION_STEP * n, 1)
                one = near_bottom * shifted_low
                two = far_bottom * shifted_low + near_top * shifted_high
                for which, value in ((0, one), (1, two)):
                    old = sums[which][n]
                    sums[which][n] = value if old is None else old + value
    values[:, : KINDS * LANES] = stats[...]
    lane = lax.rem(lax.broadcasted_iota(jnp.int32, (channels, LANES), 1), rows)
    outside = jnp.where(lane < DILATION_STEP, 1.0 - has_above, 0.0)
    outside = jnp.where(lane >= rows - DILATION_STEP, 1.0 - has_below, outside)
    at = KINDS * LANES
    for kind in (0, 5):
        values[:, at : at + LANES] = stats[:, kind * LANES : (kind + 1) * LANES] * outside
        at += LANES
    high, low = split(values[...])
    pairs = contract(high, table[...], NN) + contract(low, table[...], NN)
    lane = lax.broadcasted_iota(jnp.int32, (channels, LANES), 1)
    for which in range(2):
        pieces = [folded(sums[which][n]) for n in range(-2, 3)]
        centre = sums[which][0]
        pieces.append(jnp.where(lane < DILATION_STEP, centre[:, :LANES], 0.0))
        pieces.append(
            jnp.where(lane >= LANES - DILATION_STEP, centre[:, columns - LANES :], 0.0)
        )
        for n, piece in enumerate(pieces):
            at = which * HALO_KINDS + n
            pairs = pairs + jnp.sum(piece, axis=1, keepdims=True) * halo_table[at : at + 1, :]
    source, tap = spread()
    weights = exact(taps[...], (source // len(TAPS) == tap).astype(F32), TN)
    gathered = (source % len(TAPS) == tap).astype(F32)
    gradient[...] = exact(gathered, pairs * weights, NT) * scale


def tap_sums(flags, tops, bottoms, above, below, stats, taps, rows):
    _, _, channels, columns = tops.shape
    scale = 1.0 / (rows * lax.axis_size("space") * columns)
    table, halo_table = selection(rows)
    table = jnp.asarray(table, BF16)
    vmem = pl.BlockSpec(memory_space=pltpu.VMEM)
    smem = pl.BlockSpec(memory_space=pltpu.SMEM)

    def kernel(*refs):
        gradient_kernel(scale, rows, *refs)

    return pl.pallas_call(
        kernel,
        out_shape=jax.ShapeDtypeStruct((len(TAPS), channels), F32),
        in_specs=[smem] + [vmem] * 8,
        out_specs=vmem,
        scratch_shapes=[pltpu.VMEM((channels, table.shape[0]), F32)],
        compiler_params=SMALL,
        name="tap_sums",
    )(flags, *on_chip(tops, bottoms, above, below, stats, taps, table, jnp.asarray(halo_table)))


def beside(top, bottom, axis):
    count = lax.axis_size(axis)
    if count == 2:
        sent = jnp.where(lax.axis_index(axis) == 0, bottom, top)
        got = lax.ppermute(sent, axis, [(0, 1), (1, 0)])
        return got, got
    forward = [(i, (i + 1) % count) for i in range(count)]
    backward = [(target, source) for source, target in forward]
    return lax.ppermute(bottom, axis, forward), lax.ppermute(top, axis, backward)


def partner(value, axis):
    if lax.axis_size(axis) == 2:
        return lax.ppermute(value, axis, [(0, 1), (1, 0)])
    return lax.psum(value, axis) - value


def total(value, axis):
    if lax.axis_size(axis) == 2:
        return added(value, partner(value, axis))
    return lax.psum(value, axis)


def local(
    frames,
    conv_taps,
    pooling,
    gain_matrix,
    transition,
    update_map,
    quiet_root,
    observed_root,
    init_mean,
    init_root,
    observed,
):
    step_count, _, rows, _ = frames.shape
    place = lax.axis_index("tm").astype(jnp.int32)[None]
    flags = history(observed[None], "tm")
    tops = frames[:, :, :EDGE].transpose(0, 2, 1, 3)
    bottoms = frames[:, :, rows - EDGE :].transpose(0, 2, 1, 3)
    above, below = beside(tops[:, :DILATION_STEP], bottoms[:, DILATION_STEP:], "space")
    taps, gain = conv_taps.T, gain_matrix.T
    span = 2 if step_count % 2 == 0 else 1
    part, stats = frame_sums(taps, observed, frames, pooling)
    gain_part = gain_sums(observed, above, below, part, taps, pooling, gain)
    shifts = total(gain_part, "chan")
    gradient = tap_sums(observed, tops, bottoms, above, below, stats, taps, rows)
    shifts = total(shifts, "space")
    map_high, map_low, span_high, span_low, span_gram, first_gram = prepare(
        span, transition, update_map, quiet_root, observed_root, init_root
    )
    held = history(shifts[None], "tm")
    gradient_beside = partner(gradient, "space")
    gram = recursion(place, flags, step_count, span, span_high, span_low, span_gram, first_gram)
    tops = factor_top(gram)
    root, filtered_means, gradient = factor(
        place, flags, step_count, span, gram, tops,
        map_high, map_low, span_high, span_low, held, init_mean, gradient, gradient_beside,
    )
    return (filtered_means, root[None], gradient.transpose(1, 2, 0))


def solution(mesh):
    return jax.shard_map(
        local,
        mesh=mesh,
        in_specs=(
            P(("groups", "tm"), "chan", "space", None),
            P("chan", None),
            P("space", None),
            P(None, ("space", "chan")),
            P(),
            P(),
            P(),
            P(),
            P("groups"),
            P("groups", None),
            P(("groups", "tm")),
        ),
        out_specs=(
            P(("groups", "tm"), None),
            P(("groups", "tm"), None, None),
            P(("groups", "tm"), "chan", None),
        ),
        check_vma=False,
    )
```

```python
import math

import jax
import jax.numpy as jnp
import numpy as np
from jax import lax
from jax.experimental import pallas as pl
from jax.experimental.pallas import tpu as pltpu
from jax.sharding import PartitionSpec as P


DILATION_STEP = 2
PANEL = 32
GROUP = 8
LANES = 128
F32 = jnp.float32
BF16 = jnp.bfloat16

precise = lax.Precision.HIGHEST
SMALL = pltpu.CompilerParams(vmem_limit_bytes=16 * 2**20)


def paired(count):
    return count & (count - 1) == 0


def slot_of(block, place, count):
    return block ^ place if paired(count) else block


def join_kernel(a, b, out):
    length = a.shape[0]
    out[:length] = a[...]
    out[length:] = b[...]


def joined(a, b):
    return pl.pallas_call(
        join_kernel,
        out_shape=jax.ShapeDtypeStruct((2 * a.shape[0],) + a.shape[1:], a.dtype),
        compiler_params=SMALL,
        name="joined",
    )(*on_chip(a, b))


def add_kernel(a, b, out):
    out[...] = a[...] + b[...]


def added(a, b):
    return pl.pallas_call(
        add_kernel,
        out_shape=jax.ShapeDtypeStruct(a.shape, a.dtype),
        compiler_params=SMALL,
        name="added",
    )(*on_chip(a, b))


def packed_kernel(mine, got, gradient, out):
    steps = mine.shape[0]
    taps, channels = gradient.shape
    out[...] = jnp.zeros(out.shape, F32)
    out[:steps] = mine[...] + got[...]
    out[TAP_ROW : TAP_ROW + taps, :channels] = gradient[...]


def packed(mine, got, gradient):
    rows = TAP_ROW + -(-gradient.shape[0] // GROUP) * GROUP
    return pl.pallas_call(
        packed_kernel,
        out_shape=jax.ShapeDtypeStruct((rows, mine.shape[1]), F32),
        compiler_params=SMALL,
        name="packed",
    )(*on_chip(mine, got, gradient))


def first_sum_kernel(mine, got, out):
    steps = out.shape[1]
    out[0] = mine[:steps] + got[:steps]


def first_sum(mine, got, steps):
    return pl.pallas_call(
        first_sum_kernel,
        out_shape=jax.ShapeDtypeStruct((1, steps, mine.shape[1]), F32),
        compiler_params=SMALL,
        name="first_sum",
    )(*on_chip(mine, got))


def history(own, axis):
    count = lax.axis_size(axis)
    if not paired(count):
        return [lax.all_gather(own[0], axis)]
    pieces = [own]
    reach = 1
    while reach < count:
        sent = pieces[0]
        for piece in pieces[1:]:
            sent = joined(sent, piece)
        pieces.append(lax.ppermute(sent, axis, [(i, i ^ reach) for i in range(count)]))
        reach *= 2
    return pieces


def on_chip(*arrays):
    return [pltpu.with_memory_space_constraint(array, pltpu.VMEM) for array in arrays]


def split(x):
    high = x.astype(BF16)
    return high, (x - high.astype(F32)).astype(BF16)


def contract(a, b, dims):
    return lax.dot_general(a, b, (dims, ((), ())), preferred_element_type=F32)


def three_pass(a, b, dims):
    return (
        contract(a[0], b[0], dims)
        + contract(a[0], b[1], dims)
        + contract(a[1], b[0], dims)
    )


def exact(a, b, dims):
    return lax.dot_general(
        a, b, (dims, ((), ())), precision=precise, preferred_element_type=F32
    )


NN = ((1,), (0,))
NT = ((1,), (1,))
TN = ((0,), (0,))


def prepare_kernel(
    span, transition, update_map, quiet_root, observed_root, init_root,
    map_high, map_low, span_high, span_low, span_gram, first_gram,
):
    maps = [split(transition[...]), split(update_map[...])]
    for which, (high, low) in enumerate(maps):
        map_high[which] = high
        map_low[which] = low
    grams = []
    for ref in (quiet_root, observed_root):
        pair = split(ref[...])
        grams.append(three_pass(pair, pair, TN))
    pair = split(init_root[...])
    first_gram[...] = three_pass(pair, pair, TN)
    if span == 1:
        for which, (high, low) in enumerate(maps):
            span_high[which] = high
            span_low[which] = low
            span_gram[which] = grams[which]
        return
    for later in range(2):
        for earlier in range(2):
            which = 2 * later + earlier
            span_high[which], span_low[which] = split(
                three_pass(maps[later], maps[earlier], NN)
            )
            carried = three_pass(maps[later], split(grams[earlier]), NN)
            span_gram[which] = three_pass(split(carried), maps[later], NT) + grams[later]


def prepare(span, transition, update_map, quiet_root, observed_root, init_root):
    size = transition.shape[0]
    many = 2**span

    def kernel(*refs):
        prepare_kernel(span, *refs)

    return pl.pallas_call(
        kernel,
        out_shape=(
            pltpu.VMEM((2, size, size), BF16),
            pltpu.VMEM((2, size, size), BF16),
            pltpu.VMEM((many, size, size), BF16),
            pltpu.VMEM((many, size, size), BF16),
            pltpu.VMEM((many, size, size), F32),
            pltpu.VMEM((size, size), F32),
        ),
        compiler_params=SMALL,
        name="prepare",
    )(*on_chip(transition, update_map, quiet_root, observed_root, init_root))


def upper_factor(gram, out, high, low, begin, end, beside_work=()):
    size = gram.shape[0]
    halves = size // LANES
    tile = (GROUP, LANES)
    zero = jnp.zeros(tile, F32)
    sub = lax.broadcasted_iota(jnp.int32, tile, 0)
    lane = lax.broadcasted_iota(jnp.int32, tile, 1)
    count = PANEL // GROUP
    pending = list(beside_work)
    for top in range(begin, end, PANEL):
        first = top // LANES
        start = first * LANES
        panel = gram[top : top + PANEL, start:]
        if top:
            left = (high[:top, top : top + PANEL], low[:top, top : top + PANEL])
            panel = panel - three_pass(left, (high[:top, start:], low[:top, start:]), TN)
        places = range(halves - first)
        part = [
            [
                panel[GROUP * i : GROUP * (i + 1), LANES * h : LANES * (h + 1)]
                for h in places
            ]
            for i in range(count)
        ]
        done = [[zero for _ in places] for _ in range(count)]
        for g in range(count):
            if pending:
                pending.pop(0)()
            base = top + GROUP * g
            here, at = base // LANES - first, base % LANES
            live = range(here, halves - first)
            column = {
                i: [
                    jnp.broadcast_to(part[i][here][:, at + j : at + j + 1], tile)
                    for j in range(GROUP)
                ]
                for i in range(g, count)
            }
            pivot = {
                (j, m): jnp.broadcast_to(column[g][m][j : j + 1, :], tile)
                for j in range(GROUP)
                for m in range(j, GROUP)
            }
            factor, scale = {}, []
            for j in range(GROUP):
                scale.append(lax.rsqrt(pivot[j, j]))
                for m in range(j + 1, GROUP):
                    factor[j, m] = pivot[j, m] * scale[j]
                for i in range(j + 1, GROUP):
                    for m in range(i, GROUP):
                        pivot[i, m] = pivot[i, m] - factor[j, i] * factor[j, m]
            rows = {}
            for h in live:
                rows[h] = []
                for j in range(GROUP):
                    value = jnp.broadcast_to(part[g][h][j : j + 1, :], tile)
                    for i in range(j):
                        value = value - factor[i, j] * rows[h][i]
                    rows[h].append(value * scale[j])
                value = rows[h][0]
                for j in range(1, GROUP):
                    value = jnp.where(sub == j, rows[h][j], value)
                if h == here:
                    value = jnp.where(lane - at >= sub, value, 0.0)
                done[g][h] = value
            for i in range(g + 1, count):
                left = []
                for j in range(GROUP):
                    value = column[i][j]
                    for m in range(j):
                        value = value - factor[m, j] * left[m]
                    left.append(value * scale[j])
                for h in live:
                    value = part[i][h]
                    for j in range(GROUP):
                        value = value - left[j] * rows[h][j]
                    part[i][h] = value
        for i in range(count):
            low_row = top + GROUP * i
            for h in range(halves):
                value = done[i][h - first] if h >= first else zero
                out[low_row : low_row + GROUP, LANES * h : LANES * (h + 1)] = value
        if top + PANEL < size:
            rows_high, rows_low = split(out[top : top + PANEL, :])
            high[top : top + PANEL, :] = rows_high
            low[top : top + PANEL, :] = rows_low
    for work in pending:
        work()


def flag_reader(pieces, table):
    slot = 0
    for piece in pieces:
        for row in range(piece.shape[0]):
            for t in range(piece.shape[1]):
                table[slot + row, t] = piece[row, t]
        slot += piece.shape[0]
    return lambda slot, t: table[slot, t]


def recursion_kernel(
    steps, span, pieces, place, *refs
):
    flag_at = flag_reader(refs[:pieces], refs[-1])
    span_high, span_low, span_gram, first_gram, gram, _ = refs[pieces:]
    count = refs[-1].shape[0]
    index = place[0]
    parts = steps // span
    gram[...] = first_gram[...]

    def step(n, carry):
        slot = slot_of(n // parts, index, count)
        t = (n % parts) * span
        which = flag_at(slot, t)
        for later in range(1, span):
            which = which + flag_at(slot, t + later) * 2**later
        map_pair = (span_high[which], span_low[which])
        old = split(gram[...])
        half = gram.shape[0] // 2
        new = []
        for at in (0, half):
            left = (map_pair[0][at : at + half], map_pair[1][at : at + half])
            carried = three_pass(left, old, NN)
            new.append(
                three_pass(split(carried), map_pair, NT) + span_gram[which, at : at + half]
            )
        for n_half, at in enumerate((0, half)):
            gram[at : at + half] = new[n_half]
        return carry

    lax.fori_loop(0, (index + 1) * parts, step, 0)


def recursion(place, flags, steps, span, span_high, span_low, span_gram, first_gram):
    vmem = pl.BlockSpec(memory_space=pltpu.VMEM)
    smem = pl.BlockSpec(memory_space=pltpu.SMEM)

    def kernel(*refs):
        recursion_kernel(steps, span, len(flags), *refs)

    count = sum(piece.shape[0] for piece in flags)
    return pl.pallas_call(
        kernel,
        out_shape=pltpu.VMEM(first_gram.shape, F32),
        in_specs=[smem] * (1 + len(flags)) + [vmem] * 4,
        out_specs=vmem,
        scratch_shapes=[pltpu.SMEM((count, steps), jnp.int32)],
        compiler_params=SMALL,
        name="recursion",
    )(place, *flags, *on_chip(span_high, span_low, span_gram, first_gram))


def factor_top_kernel(gram, out, high, low):
    upper_factor(gram, out, high, low, 0, out.shape[0])


def factor_top(gram):
    size = gram.shape[0]
    rows = size // (2 * PANEL) * PANEL
    return pl.pallas_call(
        factor_top_kernel,
        out_shape=(
            pltpu.VMEM((rows, size), F32),
            pltpu.VMEM((rows, size), BF16),
            pltpu.VMEM((rows, size), BF16),
        ),
        compiler_params=SMALL,
        name="factor_top",
    )(*on_chip(gram))


def factor_kernel(
    steps, span, flag_pieces, shift_pieces, place, *refs
):
    flag_at = flag_reader(refs[:flag_pieces], refs[-1])
    gram, top, top_high, top_low, map_high, map_low = refs[flag_pieces : flag_pieces + 6]
    span_high, span_low, init_mean, gradient, gradient_beside = refs[
        flag_pieces + 6 : flag_pieces + 11
    ]
    received = refs[flag_pieces + 11 : flag_pieces + 11 + shift_pieces]
    out, mean_out, gradient_out, high, low, carried, shifts, _ = refs[
        flag_pieces + 11 + shift_pieces :
    ]
    index = place[0]
    size = gram.shape[0]
    count = shifts.shape[0]
    slot = 0
    for piece in received:
        shifts[slot : slot + piece.shape[0]] = piece[...]
        slot += piece.shape[0]
    begin = top.shape[0]
    area = (pl.ds(TAP_ROW, gradient_out.shape[0]), pl.ds(0, gradient_out.shape[2]))
    gradient_out[:, 0, :] = gradient[area] + gradient_beside[area]
    out[:begin] = top[...]
    high[:begin] = top_high[...]
    low[:begin] = top_low[...]
    state = {"mean": jnp.broadcast_to(init_mean[...], (GROUP, size))}

    def first():
        rows = split(jnp.concatenate([shifts[slot] for slot in range(count)], axis=0))
        for which in range(2):
            values = three_pass(rows, (map_high[which], map_low[which]), NT)
            for slot in range(count):
                carried[which, slot] = values[slot * steps : (slot + 1) * steps]

    def work(block, t):
        own = block == count
        slot = slot_of(index, index, count) if own else slot_of(block, index, count)

        def one_step():
            flag = flag_at(slot, t)
            mean = three_pass(split(state["mean"]), (map_high[flag], map_low[flag]), NT)
            return mean + shifts[slot, t : t + 1, :]

        def run():
            if span == 1:
                mean = one_step()
            else:
                if own:
                    mean_out[t : t + 1, :] = one_step()[0:1]
                first_flag, last_flag = flag_at(slot, t), flag_at(slot, t + 1)
                which = first_flag + 2 * last_flag
                mean = three_pass(split(state["mean"]), (span_high[which], span_low[which]), NT)
                mean = mean + carried[last_flag, slot, t : t + 1, :]
                mean = mean + shifts[slot, t + 1 : t + 2, :]
            if own:
                mean_out[t + span - 1 : t + span, :] = mean[0:1]
            else:
                mean = jnp.where(block < index, mean, state["mean"])
            state["mean"] = mean

        return run

    jobs = [first] if span == 2 else []
    blocks = list(range(count - 1)) + [count]
    jobs += [work(block, t) for block in blocks for t in range(0, steps, span)]
    upper_factor(gram, out, high, low, begin, size, jobs)


def factor(
    place, flags, steps, span, gram, tops, map_high, map_low, span_high, span_low, shifts,
    init_mean, gradient, gradient_beside, channels,
):
    size = gram.shape[0]
    taps = len(TAPS)
    count = sum(piece.shape[0] for piece in flags)
    vmem = pl.BlockSpec(memory_space=pltpu.VMEM)
    smem = pl.BlockSpec(memory_space=pltpu.SMEM)

    def kernel(*refs):
        factor_kernel(steps, span, len(flags), len(shifts), *refs)

    return pl.pallas_call(
        kernel,
        out_shape=(
            jax.ShapeDtypeStruct((size, size), F32),
            jax.ShapeDtypeStruct((steps, size), F32),
            jax.ShapeDtypeStruct((taps, 1, channels), F32),
        ),
        in_specs=[smem] * (1 + len(flags)) + [vmem] * (11 + len(shifts)),
        out_specs=(vmem, vmem, vmem),
        scratch_shapes=[
            pltpu.VMEM((size, size), BF16),
            pltpu.VMEM((size, size), BF16),
            pltpu.VMEM((2, count, steps, size), F32),
            pltpu.VMEM((count, steps, size), F32),
            pltpu.SMEM((count, steps), jnp.int32),
        ],
        compiler_params=SMALL,
        name="factor",
    )(
        place,
        *flags,
        *on_chip(
            gram, *tops, map_high, map_low, span_high, span_low, init_mean[None],
            gradient, gradient_beside, *shifts,
        ),
    )


LAGS = (0, DILATION_STEP, 2 * DILATION_STEP, -DILATION_STEP, -2 * DILATION_STEP)
TAPS = tuple((a, b) for a in (-1, 0, 1) for b in (-1, 0, 1))
EDGE = 2 * DILATION_STEP
KINDS = 8
TAP_ROW = 8
EDGE_KINDS = 2
HALO_KINDS = 7


def moved(x, by, axis):
    if by == 0:
        return x
    length = x.shape[axis]
    shape = list(x.shape)
    shape[axis] = abs(by)
    zeros = jnp.zeros(shape, x.dtype)
    if by > 0:
        return jnp.concatenate(
            [lax.slice_in_dim(x, by, length, axis=axis), zeros], axis=axis
        )
    return jnp.concatenate(
        [zeros, lax.slice_in_dim(x, 0, length + by, axis=axis)], axis=axis
    )


def folded(x):
    total = x[:, :LANES]
    for at in range(LANES, x.shape[1], LANES):
        total = total + x[:, at : at + LANES]
    return total


def frames_kernel(
    unroll, taps, flags, source, pooling, part, stats, pooled, frames, arrived
):
    steps, channels, rows, columns = frames.shape
    copies = []
    for n in range(channels // unroll):
        piece = (slice(None), pl.ds(n * unroll, unroll))
        copies.append(
            pltpu.make_async_copy(source.at[piece], frames.at[piece], arrived.at[n])
        )
        copies[-1].start()
    for k, (a, b) in enumerate(TAPS):
        pooled[k] = moved(
            moved(pooling[...], -DILATION_STEP * b, 1), -DILATION_STEP * a, 0
        )
    lane = lax.broadcasted_iota(jnp.int32, (rows, LANES), 1)
    row = lax.broadcasted_iota(jnp.int32, (rows, LANES), 0)
    masks = [lax.rem(lane, rows) - row == lag for lag in LAGS]
    left_edge = (lane < DILATION_STEP).astype(F32).astype(BF16)
    right_edge = (lane >= LANES - DILATION_STEP).astype(F32).astype(BF16)
    left_half = (lane < LANES // 2).astype(F32).astype(BF16)
    right_half = (lane >= LANES // 2).astype(F32).astype(BF16)
    middle = LANES // 2 - DILATION_STEP
    blank = jnp.zeros((LANES - 3 * rows, columns), BF16)
    edge_blank = jnp.zeros((LANES - 2 * rows, LANES), BF16)

    def channel(c):
        weights = taps[0, c] * pooled[0]
        for k in range(1, len(TAPS)):
            weights = weights + taps[k, c] * pooled[k]
        gram = jnp.zeros((rows, LANES), F32)
        borders = jnp.zeros((rows, LANES), BF16)
        for t in range(steps):
            frame = frames[t, c]
            part[t, pl.ds(c, 1), :] = jnp.sum(
                folded(frame.astype(F32) * weights), axis=0, keepdims=True
            )
            partners = jnp.concatenate(
                [
                    frame,
                    moved(frame, DILATION_STEP, 1),
                    moved(frame, 2 * DILATION_STEP, 1),
                    blank,
                ],
                axis=0,
            )
            seen = frame * flags[t].astype(F32).astype(BF16)
            gram = gram + contract(seen, partners, NT)
            at = DILATION_STEP * t
            borders = borders + moved(seen[:, :LANES] * left_edge, -at, 1)
            borders = borders + moved(seen[:, columns - LANES :] * right_edge, middle - at, 1)
        edge = contract(
            borders,
            jnp.concatenate([borders * left_half, borders * right_half, edge_blank], axis=0),
            NT,
        )
        sums = [jnp.sum(jnp.where(m, gram, 0.0), axis=0, keepdims=True) for m in masks]
        sums += [jnp.sum(jnp.where(m, edge, 0.0), axis=0, keepdims=True) for m in masks[:3]]
        stats[pl.ds(c, 1), :] = jnp.concatenate(sums, axis=1)

    def several(n, carry):
        piece = (slice(None), pl.ds(n * unroll, unroll))
        pltpu.make_async_copy(source.at[piece], frames.at[piece], arrived.at[n]).wait()
        for u in range(unroll):
            channel(n * unroll + u)
        return carry

    lax.fori_loop(0, channels // unroll, several, 0)


def frame_sums(taps, flags, frames, pooling):
    steps, channels, rows, columns = frames.shape
    vmem = pl.BlockSpec(memory_space=pltpu.VMEM)
    smem = pl.BlockSpec(memory_space=pltpu.SMEM)

    unroll = math.gcd(channels, 16)

    def kernel(*refs):
        frames_kernel(unroll, *refs)

    return pl.pallas_call(
        kernel,
        out_shape=(
            pltpu.VMEM((steps, channels, LANES), F32),
            pltpu.VMEM((channels, KINDS * LANES), F32),
        ),
        in_specs=[smem, smem, pl.BlockSpec(memory_space=pltpu.HBM), vmem],
        out_specs=(vmem, vmem),
        scratch_shapes=[
            pltpu.VMEM((len(TAPS), rows, columns), F32),
            pltpu.VMEM(frames.shape, frames.dtype),
            pltpu.SemaphoreType.DMA((channels // unroll,)),
        ],
        compiler_params=SMALL,
        name="frame_sums",
    )(
        taps, flags, pltpu.with_memory_space_constraint(frames, pltpu.HBM), *on_chip(pooling)
    )


def selection(rows):
    near = np.zeros((KINDS, LANES, len(TAPS), len(TAPS)), np.float32)
    edge = np.zeros((EDGE_KINDS, LANES, len(TAPS), len(TAPS)), np.float32)
    halo = np.zeros((2, HALO_KINDS, len(TAPS), len(TAPS)), np.float32)
    own = np.arange(rows)
    top, bottom = own[:DILATION_STEP], own[rows - DILATION_STEP :]
    for i, (a, b) in enumerate(TAPS):
        for j, (c, d) in enumerate(TAPS):
            down, across = c - a, d - b
            if (down, across) < (0, 0):
                down, across = -down, -across
            lag = abs(across)
            kind = down if across >= 0 else down + 2
            near[kind, lag * rows + own, i, j] += 1
            if down:
                halo[down - 1, across + 2, i, j] += 1
            for side, group in ((1, 0), (-1, 1)):
                if b == d == side:
                    near[5 + down, group * rows + own, i, j] -= 1
                    if down:
                        halo[down - 1, 5 + group, i, j] -= 1
            if a == c != 0:
                lost = top if a == 1 else bottom
                edge[0, lag * rows + lost, i, j] -= 1
                for side, group in ((1, 0), (-1, 1)):
                    if b == d == side:
                        edge[1, group * rows + lost, i, j] += 1
    pairs = len(TAPS) ** 2
    table = np.concatenate([m.reshape(-1, pairs) for m in (near, edge)], axis=0)
    halo = np.pad(halo.reshape(-1, pairs), ((0, -2 * HALO_KINDS % GROUP), (0, 0)))
    return [np.pad(m, ((0, 0), (0, LANES - pairs))) for m in (table, halo)]


def beside_tile():
    place, count = lax.axis_index("space"), lax.axis_size("space")
    has_above = jnp.where(place > 0, 1.0, 0.0).astype(F32)
    has_below = jnp.where(place < count - 1, 1.0, 0.0).astype(F32)
    return has_above, has_below


def spread():
    shape = (len(TAPS), LANES)
    source = lax.broadcasted_iota(jnp.int32, shape, 1)
    return source, lax.broadcasted_iota(jnp.int32, shape, 0)


def gain_kernel(flags, above, below, part, taps, pooling, gain, gain_part):
    steps, _, channels, columns = above.shape
    rows = pooling.shape[0]
    has_above, has_below = beside_tile()
    source, tap = spread()
    tap_columns = exact(taps[...], (source == tap).astype(F32), TN)
    halo_weights = []
    for a, start, has in ((-1, 0, has_above), (1, rows - DILATION_STEP, has_below)):
        for r in range(DILATION_STEP):
            value = jnp.zeros((channels, columns), F32)
            for b in (-1, 0, 1):
                k = TAPS.index((a, b))
                shifted = moved(pooling[start + r : start + r + 1, :], -DILATION_STEP * b, 1)
                value = value + tap_columns[:, k : k + 1] * shifted
            halo_weights.append(value * has)
    row_sums = []
    for t in range(steps):
        total = jnp.zeros((channels, columns), F32)
        for r in range(DILATION_STEP):
            total = total + above[t, r].astype(F32) * halo_weights[r]
            total = total + below[t, r].astype(F32) * halo_weights[DILATION_STEP + r]
        row_sums.append(part[t] + folded(total))
    ones = jnp.ones((GROUP, LANES), BF16)
    high, low = split(jnp.concatenate(row_sums, axis=0))
    tile_sums = contract(ones, high, NT) + contract(ones, low, NT)
    shape = (GROUP, steps * channels)
    owner = lax.broadcasted_iota(jnp.int32, shape, 1) // channels
    step = lax.broadcasted_iota(jnp.int32, shape, 0)
    seen = jnp.zeros(shape, F32)
    for t in range(steps):
        seen = jnp.where((owner == t) & (step == t), flags[t].astype(F32), seen)
    gains = jnp.concatenate([gain[...]] * steps, axis=0)
    product = three_pass(split(tile_sums * seen), split(gains), NN)
    gain_part[...] = product[:steps]


def gain_sums(flags, above, below, part, taps, pooling, gain):
    vmem = pl.BlockSpec(memory_space=pltpu.VMEM)
    smem = pl.BlockSpec(memory_space=pltpu.SMEM)
    return pl.pallas_call(
        gain_kernel,
        out_shape=jax.ShapeDtypeStruct((above.shape[0], gain.shape[1]), F32),
        in_specs=[smem] + [vmem] * 6,
        out_specs=vmem,
        compiler_params=SMALL,
        name="gain_sums",
    )(flags, *on_chip(above, below, part, taps, pooling, gain))


def gradient_kernel(
    scale, rows, flags, tops, bottoms, above, below, stats, taps, table, halo_table,
    gradient, values,
):
    steps, _, channels, columns = tops.shape
    has_above, has_below = beside_tile()
    sums = [[None] * 5 for _ in range(2)]
    for t in range(steps):
        flag = flags[t].astype(F32)
        for r in range(DILATION_STEP):
            near_top = tops[t, DILATION_STEP + r].astype(F32)
            far_bottom = bottoms[t, r].astype(F32)
            near_bottom = bottoms[t, DILATION_STEP + r].astype(F32)
            high = above[t, r].astype(F32) * (flag * has_above)
            low = below[t, r].astype(F32) * (flag * has_below)
            for n in range(-2, 3):
                shifted_low = moved(low, DILATION_STEP * n, 1)
                shifted_high = moved(high, -DILATION_STEP * n, 1)
                one = near_bottom * shifted_low
                two = far_bottom * shifted_low + near_top * shifted_high
                for which, value in ((0, one), (1, two)):
                    old = sums[which][n]
                    sums[which][n] = value if old is None else old + value
    values[:, : KINDS * LANES] = stats[...]
    lane = lax.rem(lax.broadcasted_iota(jnp.int32, (channels, LANES), 1), rows)
    outside = jnp.where(lane < DILATION_STEP, 1.0 - has_above, 0.0)
    outside = jnp.where(lane >= rows - DILATION_STEP, 1.0 - has_below, outside)
    at = KINDS * LANES
    for kind in (0, 5):
        values[:, at : at + LANES] = stats[:, kind * LANES : (kind + 1) * LANES] * outside
        at += LANES
    high, low = split(values[...])
    pairs = contract(high, table[...], NN) + contract(low, table[...], NN)
    lane = lax.broadcasted_iota(jnp.int32, (channels, LANES), 1)
    for which in range(2):
        pieces = [folded(sums[which][n]) for n in range(-2, 3)]
        centre = sums[which][0]
        pieces.append(jnp.where(lane < DILATION_STEP, centre[:, :LANES], 0.0))
        pieces.append(
            jnp.where(lane >= LANES - DILATION_STEP, centre[:, columns - LANES :], 0.0)
        )
        for n, piece in enumerate(pieces):
            at = which * HALO_KINDS + n
            pairs = pairs + jnp.sum(piece, axis=1, keepdims=True) * halo_table[at : at + 1, :]
    source, tap = spread()
    weights = exact(taps[...], (source // len(TAPS) == tap).astype(F32), TN)
    gathered = (source % len(TAPS) == tap).astype(F32)
    gradient[...] = exact(gathered, pairs * weights, NT) * scale


def tap_sums(flags, tops, bottoms, above, below, stats, taps, rows):
    _, _, channels, columns = tops.shape
    scale = 1.0 / (rows * lax.axis_size("space") * columns)
    table, halo_table = selection(rows)
    table = jnp.asarray(table, BF16)
    vmem = pl.BlockSpec(memory_space=pltpu.VMEM)
    smem = pl.BlockSpec(memory_space=pltpu.SMEM)

    def kernel(*refs):
        gradient_kernel(scale, rows, *refs)

    return pl.pallas_call(
        kernel,
        out_shape=jax.ShapeDtypeStruct((len(TAPS), channels), F32),
        in_specs=[smem] + [vmem] * 8,
        out_specs=vmem,
        scratch_shapes=[pltpu.VMEM((channels, table.shape[0]), F32)],
        compiler_params=SMALL,
        name="tap_sums",
    )(flags, *on_chip(tops, bottoms, above, below, stats, taps, table, jnp.asarray(halo_table)))


def beside(top, bottom, axis):
    count = lax.axis_size(axis)
    if count == 2:
        sent = jnp.where(lax.axis_index(axis) == 0, bottom, top)
        got = lax.ppermute(sent, axis, [(0, 1), (1, 0)])
        return got, got
    forward = [(i, (i + 1) % count) for i in range(count)]
    backward = [(target, source) for source, target in forward]
    return lax.ppermute(bottom, axis, forward), lax.ppermute(top, axis, backward)


def partner(value, axis):
    if lax.axis_size(axis) == 2:
        return lax.ppermute(value, axis, [(0, 1), (1, 0)])
    return lax.psum(value, axis) - value


def total(value, axis):
    if lax.axis_size(axis) == 2:
        return added(value, partner(value, axis))
    return lax.psum(value, axis)


def local(
    frames,
    conv_taps,
    pooling,
    gain_matrix,
    transition,
    update_map,
    quiet_root,
    observed_root,
    init_mean,
    init_root,
    observed,
):
    step_count, channels, rows, _ = frames.shape
    place = lax.axis_index("tm").astype(jnp.int32)[None]
    flags = history(observed[None], "tm")
    tops = frames[:, :, :EDGE].transpose(0, 2, 1, 3)
    bottoms = frames[:, :, rows - EDGE :].transpose(0, 2, 1, 3)
    above, below = beside(tops[:, :DILATION_STEP], bottoms[:, DILATION_STEP:], "space")
    taps, gain = conv_taps.T, gain_matrix.T
    span = 2 if step_count % 2 == 0 else 1
    part, stats = frame_sums(taps, observed, frames, pooling)
    gain_part = gain_sums(observed, above, below, part, taps, pooling, gain)
    gradient = tap_sums(observed, tops, bottoms, above, below, stats, taps, rows)
    map_high, map_low, span_high, span_low, span_gram, first_gram = prepare(
        span, transition, update_map, quiet_root, observed_root, init_root
    )
    if lax.axis_size("chan") == 2 and step_count <= TAP_ROW:
        both = packed(gain_part, partner(gain_part, "chan"), gradient)
        both_beside = partner(both, "space")
        shifts = first_sum(both, both_beside, step_count)
    else:
        both = jnp.pad(
            gradient,
            ((TAP_ROW, 2 * GROUP - len(TAPS)), (0, gain.shape[1] - channels)),
        )
        shifts = total(total(gain_part, "chan"), "space")[None]
        both_beside = partner(both, "space")
    held = history(shifts, "tm")
    gram = recursion(place, flags, step_count, span, span_high, span_low, span_gram, first_gram)
    tops = factor_top(gram)
    root, filtered_means, gradient = factor(
        place, flags, step_count, span, gram, tops,
        map_high, map_low, span_high, span_low, held, init_mean, both, both_beside, channels,
    )
    return (filtered_means, root[None], gradient.transpose(1, 2, 0))


def solution(mesh):
    return jax.shard_map(
        local,
        mesh=mesh,
        in_specs=(
            P(("groups", "tm"), "chan", "space", None),
            P("chan", None),
            P("space", None),
            P(None, ("space", "chan")),
            P(),
            P(),
            P(),
            P(),
            P("groups"),
            P("groups", None),
            P(("groups", "tm")),
        ),
        out_specs=(
            P(("groups", "tm"), None),
            P(("groups", "tm"), None, None),
            P(("groups", "tm"), "chan", None),
        ),
        check_vma=False,
    )
```

```python
import math

import jax
import jax.numpy as jnp
import numpy as np
from jax import lax
from jax.experimental import pallas as pl
from jax.experimental.pallas import tpu as pltpu
from jax.sharding import PartitionSpec as P


DILATION_STEP = 2
PANEL = 32
GROUP = 8
LANES = 128
F32 = jnp.float32
BF16 = jnp.bfloat16

precise = lax.Precision.HIGHEST
SMALL = pltpu.CompilerParams(vmem_limit_bytes=16 * 2**20)


def paired(count):
    return count & (count - 1) == 0


def slot_of(block, place, count):
    return block ^ place if paired(count) else block


def join_kernel(a, b, out):
    length = a.shape[0]
    out[:length] = a[...]
    out[length:] = b[...]


def joined(a, b):
    return pl.pallas_call(
        join_kernel,
        out_shape=jax.ShapeDtypeStruct((2 * a.shape[0],) + a.shape[1:], a.dtype),
        compiler_params=SMALL,
        name="joined",
    )(*on_chip(a, b))


def add_kernel(a, b, out):
    out[...] = a[...] + b[...]


def added(a, b):
    return pl.pallas_call(
        add_kernel,
        out_shape=jax.ShapeDtypeStruct(a.shape, a.dtype),
        compiler_params=SMALL,
        name="added",
    )(*on_chip(a, b))


def packed_kernel(mine, got, gradient, out):
    steps = mine.shape[0]
    taps, channels = gradient.shape
    out[...] = jnp.zeros(out.shape, F32)
    out[:steps] = mine[...] + got[...]
    out[TAP_ROW : TAP_ROW + taps, :channels] = gradient[...]


def packed(mine, got, gradient):
    rows = TAP_ROW + -(-gradient.shape[0] // GROUP) * GROUP
    return pl.pallas_call(
        packed_kernel,
        out_shape=jax.ShapeDtypeStruct((rows, mine.shape[1]), F32),
        compiler_params=SMALL,
        name="packed",
    )(*on_chip(mine, got, gradient))


def first_sum_kernel(mine, got, out):
    steps = out.shape[1]
    out[0] = mine[:steps] + got[:steps]


def first_sum(mine, got, steps):
    return pl.pallas_call(
        first_sum_kernel,
        out_shape=jax.ShapeDtypeStruct((1, steps, mine.shape[1]), F32),
        compiler_params=SMALL,
        name="first_sum",
    )(*on_chip(mine, got))


def history(own, axis):
    count = lax.axis_size(axis)
    if not paired(count):
        return [lax.all_gather(own[0], axis)]
    pieces = [own]
    reach = 1
    while reach < count:
        sent = pieces[0]
        for piece in pieces[1:]:
            sent = joined(sent, piece)
        pieces.append(lax.ppermute(sent, axis, [(i, i ^ reach) for i in range(count)]))
        reach *= 2
    return pieces


def on_chip(*arrays):
    return [pltpu.with_memory_space_constraint(array, pltpu.VMEM) for array in arrays]


def split(x):
    high = x.astype(BF16)
    return high, (x - high.astype(F32)).astype(BF16)


def contract(a, b, dims):
    return lax.dot_general(a, b, (dims, ((), ())), preferred_element_type=F32)


def three_pass(a, b, dims):
    return (
        contract(a[0], b[0], dims)
        + contract(a[0], b[1], dims)
        + contract(a[1], b[0], dims)
    )


def exact(a, b, dims):
    return lax.dot_general(
        a, b, (dims, ((), ())), precision=precise, preferred_element_type=F32
    )


NN = ((1,), (0,))
NT = ((1,), (1,))
TN = ((0,), (0,))


def prepare_kernel(
    span, transition, update_map, quiet_root, observed_root, init_root,
    map_high, map_low, span_high, span_low, span_gram, first_gram,
):
    maps = [split(transition[...]), split(update_map[...])]
    for which, (high, low) in enumerate(maps):
        map_high[which] = high
        map_low[which] = low
    grams = []
    for ref in (quiet_root, observed_root):
        pair = split(ref[...])
        grams.append(three_pass(pair, pair, TN))
    pair = split(init_root[...])
    first_gram[...] = three_pass(pair, pair, TN)
    if span == 1:
        for which, (high, low) in enumerate(maps):
            span_high[which] = high
            span_low[which] = low
            span_gram[which] = grams[which]
        return
    for later in range(2):
        for earlier in range(2):
            which = 2 * later + earlier
            span_high[which], span_low[which] = split(
                three_pass(maps[later], maps[earlier], NN)
            )
            carried = three_pass(maps[later], split(grams[earlier]), NN)
            span_gram[which] = three_pass(split(carried), maps[later], NT) + grams[later]


def prepare(span, transition, update_map, quiet_root, observed_root, init_root):
    size = transition.shape[0]
    many = 2**span

    def kernel(*refs):
        prepare_kernel(span, *refs)

    return pl.pallas_call(
        kernel,
        out_shape=(
            pltpu.VMEM((2, size, size), BF16),
            pltpu.VMEM((2, size, size), BF16),
            pltpu.VMEM((many, size, size), BF16),
            pltpu.VMEM((many, size, size), BF16),
            pltpu.VMEM((many, size, size), F32),
            pltpu.VMEM((size, size), F32),
        ),
        compiler_params=SMALL,
        name="prepare",
    )(*on_chip(transition, update_map, quiet_root, observed_root, init_root))


def upper_factor(gram, out, high, low, begin, end, beside_work=()):
    size = gram.shape[0]
    halves = size // LANES
    tile = (GROUP, LANES)
    zero = jnp.zeros(tile, F32)
    sub = lax.broadcasted_iota(jnp.int32, tile, 0)
    lane = lax.broadcasted_iota(jnp.int32, tile, 1)
    count = PANEL // GROUP
    pending = list(beside_work)
    for top in range(begin, end, PANEL):
        first = top // LANES
        start = first * LANES
        panel = gram[top : top + PANEL, start:]
        if top:
            for rows in (slice(0, top - PANEL), slice(top - PANEL, top)):
                if rows.stop:
                    left = (high[rows, top : top + PANEL], low[rows, top : top + PANEL])
                    right = (high[rows, start:], low[rows, start:])
                    panel = panel - three_pass(left, right, TN)
        places = range(halves - first)
        part = [
            [
                panel[GROUP * i : GROUP * (i + 1), LANES * h : LANES * (h + 1)]
                for h in places
            ]
            for i in range(count)
        ]
        done = [[zero for _ in places] for _ in range(count)]
        for g in range(count):
            if pending:
                pending.pop(0)()
            base = top + GROUP * g
            here, at = base // LANES - first, base % LANES
            live = range(here, halves - first)
            column = {
                i: [
                    jnp.broadcast_to(part[i][here][:, at + j : at + j + 1], tile)
                    for j in range(GROUP)
                ]
                for i in range(g, count)
            }
            pivot = {
                (j, m): jnp.broadcast_to(column[g][m][j : j + 1, :], tile)
                for j in range(GROUP)
                for m in range(j, GROUP)
            }
            factor, scale = {}, []
            for j in range(GROUP):
                scale.append(lax.rsqrt(pivot[j, j]))
                for m in range(j + 1, GROUP):
                    factor[j, m] = pivot[j, m] * scale[j]
                for i in range(j + 1, GROUP):
                    for m in range(i, GROUP):
                        pivot[i, m] = pivot[i, m] - factor[j, i] * factor[j, m]
            rows = {}
            for h in live:
                rows[h] = []
                for j in range(GROUP):
                    value = jnp.broadcast_to(part[g][h][j : j + 1, :], tile)
                    for i in range(j):
                        value = value - factor[i, j] * rows[h][i]
                    rows[h].append(value * scale[j])
                value = rows[h][0]
                for j in range(1, GROUP):
                    value = jnp.where(sub == j, rows[h][j], value)
                if h == here:
                    value = jnp.where(lane - at >= sub, value, 0.0)
                done[g][h] = value
            for i in range(g + 1, count):
                left = []
                for j in range(GROUP):
                    value = column[i][j]
                    for m in range(j):
                        value = value - factor[m, j] * left[m]
                    left.append(value * scale[j])
                for h in live:
                    value = part[i][h]
                    for j in range(GROUP):
                        value = value - left[j] * rows[h][j]
                    part[i][h] = value
        for i in range(count):
            low_row = top + GROUP * i
            for h in range(halves):
                value = done[i][h - first] if h >= first else zero
                out[low_row : low_row + GROUP, LANES * h : LANES * (h + 1)] = value
        if top + PANEL < size:
            rows_high, rows_low = split(out[top : top + PANEL, :])
            high[top : top + PANEL, :] = rows_high
            low[top : top + PANEL, :] = rows_low
    for work in pending:
        work()


def flag_reader(pieces, table):
    slot = 0
    for piece in pieces:
        for row in range(piece.shape[0]):
            for t in range(piece.shape[1]):
                table[slot + row, t] = piece[row, t]
        slot += piece.shape[0]
    return lambda slot, t: table[slot, t]


def recursion_kernel(
    steps, span, pieces, place, *refs
):
    flag_at = flag_reader(refs[:pieces], refs[-1])
    span_high, span_low, span_gram, first_gram, gram, _ = refs[pieces:]
    count = refs[-1].shape[0]
    index = place[0]
    parts = steps // span
    gram[...] = first_gram[...]

    def step(n, carry):
        slot = slot_of(n // parts, index, count)
        t = (n % parts) * span
        which = flag_at(slot, t)
        for later in range(1, span):
            which = which + flag_at(slot, t + later) * 2**later
        map_pair = (span_high[which], span_low[which])
        old = split(gram[...])
        half = gram.shape[0] // 2
        new = []
        for at in (0, half):
            left = (map_pair[0][at : at + half], map_pair[1][at : at + half])
            carried = three_pass(left, old, NN)
            new.append(
                three_pass(split(carried), map_pair, NT) + span_gram[which, at : at + half]
            )
        for n_half, at in enumerate((0, half)):
            gram[at : at + half] = new[n_half]
        return carry

    lax.fori_loop(0, (index + 1) * parts, step, 0)


def recursion(place, flags, steps, span, span_high, span_low, span_gram, first_gram):
    vmem = pl.BlockSpec(memory_space=pltpu.VMEM)
    smem = pl.BlockSpec(memory_space=pltpu.SMEM)

    def kernel(*refs):
        recursion_kernel(steps, span, len(flags), *refs)

    count = sum(piece.shape[0] for piece in flags)
    return pl.pallas_call(
        kernel,
        out_shape=pltpu.VMEM(first_gram.shape, F32),
        in_specs=[smem] * (1 + len(flags)) + [vmem] * 4,
        out_specs=vmem,
        scratch_shapes=[pltpu.SMEM((count, steps), jnp.int32)],
        compiler_params=SMALL,
        name="recursion",
    )(place, *flags, *on_chip(span_high, span_low, span_gram, first_gram))


def factor_top_kernel(gram, out, high, low):
    upper_factor(gram, out, high, low, 0, out.shape[0])


def factor_top(gram):
    size = gram.shape[0]
    rows = size // (2 * PANEL) * PANEL
    return pl.pallas_call(
        factor_top_kernel,
        out_shape=(
            pltpu.VMEM((rows, size), F32),
            pltpu.VMEM((rows, size), BF16),
            pltpu.VMEM((rows, size), BF16),
        ),
        compiler_params=SMALL,
        name="factor_top",
    )(*on_chip(gram))


def factor_kernel(
    steps, span, flag_pieces, shift_pieces, place, *refs
):
    flag_at = flag_reader(refs[:flag_pieces], refs[-1])
    gram, top, top_high, top_low, map_high, map_low = refs[flag_pieces : flag_pieces + 6]
    span_high, span_low, init_mean, gradient, gradient_beside = refs[
        flag_pieces + 6 : flag_pieces + 11
    ]
    received = refs[flag_pieces + 11 : flag_pieces + 11 + shift_pieces]
    out, mean_out, gradient_out, high, low, carried, shifts, _ = refs[
        flag_pieces + 11 + shift_pieces :
    ]
    index = place[0]
    size = gram.shape[0]
    count = shifts.shape[0]
    slot = 0
    for piece in received:
        shifts[slot : slot + piece.shape[0]] = piece[...]
        slot += piece.shape[0]
    begin = top.shape[0]
    area = (pl.ds(TAP_ROW, gradient_out.shape[0]), pl.ds(0, gradient_out.shape[2]))
    gradient_out[:, 0, :] = gradient[area] + gradient_beside[area]
    out[:begin] = top[...]
    high[:begin] = top_high[...]
    low[:begin] = top_low[...]
    state = {"mean": jnp.broadcast_to(init_mean[...], (GROUP, size))}

    def first():
        rows = split(jnp.concatenate([shifts[slot] for slot in range(count)], axis=0))
        for which in range(2):
            values = three_pass(rows, (map_high[which], map_low[which]), NT)
            for slot in range(count):
                carried[which, slot] = values[slot * steps : (slot + 1) * steps]

    def work(block, t):
        own = block == count
        slot = slot_of(index, index, count) if own else slot_of(block, index, count)

        def one_step():
            flag = flag_at(slot, t)
            mean = three_pass(split(state["mean"]), (map_high[flag], map_low[flag]), NT)
            return mean + shifts[slot, t : t + 1, :]

        def run():
            if span == 1:
                mean = one_step()
            else:
                if own:
                    mean_out[t : t + 1, :] = one_step()[0:1]
                first_flag, last_flag = flag_at(slot, t), flag_at(slot, t + 1)
                which = first_flag + 2 * last_flag
                mean = three_pass(split(state["mean"]), (span_high[which], span_low[which]), NT)
                mean = mean + carried[last_flag, slot, t : t + 1, :]
                mean = mean + shifts[slot, t + 1 : t + 2, :]
            if own:
                mean_out[t + span - 1 : t + span, :] = mean[0:1]
            else:
                mean = jnp.where(block < index, mean, state["mean"])
            state["mean"] = mean

        return run

    jobs = [first] if span == 2 else []
    blocks = list(range(count - 1)) + [count]
    jobs += [work(block, t) for block in blocks for t in range(0, steps, span)]
    upper_factor(gram, out, high, low, begin, size, jobs)


def factor(
    place, flags, steps, span, gram, tops, map_high, map_low, span_high, span_low, shifts,
    init_mean, gradient, gradient_beside, channels,
):
    size = gram.shape[0]
    taps = len(TAPS)
    count = sum(piece.shape[0] for piece in flags)
    vmem = pl.BlockSpec(memory_space=pltpu.VMEM)
    smem = pl.BlockSpec(memory_space=pltpu.SMEM)

    def kernel(*refs):
        factor_kernel(steps, span, len(flags), len(shifts), *refs)

    return pl.pallas_call(
        kernel,
        out_shape=(
            jax.ShapeDtypeStruct((size, size), F32),
            jax.ShapeDtypeStruct((steps, size), F32),
            jax.ShapeDtypeStruct((taps, 1, channels), F32),
        ),
        in_specs=[smem] * (1 + len(flags)) + [vmem] * (11 + len(shifts)),
        out_specs=(vmem, vmem, vmem),
        scratch_shapes=[
            pltpu.VMEM((size, size), BF16),
            pltpu.VMEM((size, size), BF16),
            pltpu.VMEM((2, count, steps, size), F32),
            pltpu.VMEM((count, steps, size), F32),
            pltpu.SMEM((count, steps), jnp.int32),
        ],
        compiler_params=SMALL,
        name="factor",
    )(
        place,
        *flags,
        *on_chip(
            gram, *tops, map_high, map_low, span_high, span_low, init_mean[None],
            gradient, gradient_beside, *shifts,
        ),
    )


LAGS = (0, DILATION_STEP, 2 * DILATION_STEP, -DILATION_STEP, -2 * DILATION_STEP)
TAPS = tuple((a, b) for a in (-1, 0, 1) for b in (-1, 0, 1))
EDGE = 2 * DILATION_STEP
KINDS = 8
TAP_ROW = 8
EDGE_KINDS = 2
HALO_KINDS = 7


def moved(x, by, axis):
    if by == 0:
        return x
    length = x.shape[axis]
    shape = list(x.shape)
    shape[axis] = abs(by)
    zeros = jnp.zeros(shape, x.dtype)
    if by > 0:
        return jnp.concatenate(
            [lax.slice_in_dim(x, by, length, axis=axis), zeros], axis=axis
        )
    return jnp.concatenate(
        [zeros, lax.slice_in_dim(x, 0, length + by, axis=axis)], axis=axis
    )


def folded(x):
    total = x[:, :LANES]
    for at in range(LANES, x.shape[1], LANES):
        total = total + x[:, at : at + LANES]
    return total


def frames_kernel(
    unroll, taps, flags, source, pooling, part, stats, pooled, frames, arrived
):
    steps, channels, rows, columns = frames.shape
    copies = []
    for n in range(channels // unroll):
        piece = (slice(None), pl.ds(n * unroll, unroll))
        copies.append(
            pltpu.make_async_copy(source.at[piece], frames.at[piece], arrived.at[n])
        )
        copies[-1].start()
    for k, (a, b) in enumerate(TAPS):
        pooled[k] = moved(
            moved(pooling[...], -DILATION_STEP * b, 1), -DILATION_STEP * a, 0
        )
    lane = lax.broadcasted_iota(jnp.int32, (rows, LANES), 1)
    row = lax.broadcasted_iota(jnp.int32, (rows, LANES), 0)
    masks = [lax.rem(lane, rows) - row == lag for lag in LAGS]
    left_edge = (lane < DILATION_STEP).astype(F32).astype(BF16)
    right_edge = (lane >= LANES - DILATION_STEP).astype(F32).astype(BF16)
    left_half = (lane < LANES // 2).astype(F32).astype(BF16)
    right_half = (lane >= LANES // 2).astype(F32).astype(BF16)
    middle = LANES // 2 - DILATION_STEP
    blank = jnp.zeros((LANES - 3 * rows, columns), BF16)
    edge_blank = jnp.zeros((LANES - 2 * rows, LANES), BF16)

    def channel(c):
        weights = taps[0, c] * pooled[0]
        for k in range(1, len(TAPS)):
            weights = weights + taps[k, c] * pooled[k]
        gram = jnp.zeros((rows, LANES), F32)
        borders = jnp.zeros((rows, LANES), BF16)
        for t in range(steps):
            frame = frames[t, c]
            part[t, pl.ds(c, 1), :] = jnp.sum(
                folded(frame.astype(F32) * weights), axis=0, keepdims=True
            )
            partners = jnp.concatenate(
                [
                    frame,
                    moved(frame, DILATION_STEP, 1),
                    moved(frame, 2 * DILATION_STEP, 1),
                    blank,
                ],
                axis=0,
            )
            seen = frame * flags[t].astype(F32).astype(BF16)
            gram = gram + contract(seen, partners, NT)
            at = DILATION_STEP * t
            borders = borders + moved(seen[:, :LANES] * left_edge, -at, 1)
            borders = borders + moved(seen[:, columns - LANES :] * right_edge, middle - at, 1)
        edge = contract(
            borders,
            jnp.concatenate([borders * left_half, borders * right_half, edge_blank], axis=0),
            NT,
        )
        sums = [jnp.sum(jnp.where(m, gram, 0.0), axis=0, keepdims=True) for m in masks]
        sums += [jnp.sum(jnp.where(m, edge, 0.0), axis=0, keepdims=True) for m in masks[:3]]
        stats[pl.ds(c, 1), :] = jnp.concatenate(sums, axis=1)

    def several(n, carry):
        piece = (slice(None), pl.ds(n * unroll, unroll))
        pltpu.make_async_copy(source.at[piece], frames.at[piece], arrived.at[n]).wait()
        for u in range(unroll):
            channel(n * unroll + u)
        return carry

    lax.fori_loop(0, channels // unroll, several, 0)


def frame_sums(taps, flags, frames, pooling):
    steps, channels, rows, columns = frames.shape
    vmem = pl.BlockSpec(memory_space=pltpu.VMEM)
    smem = pl.BlockSpec(memory_space=pltpu.SMEM)

    unroll = math.gcd(channels, 16)

    def kernel(*refs):
        frames_kernel(unroll, *refs)

    return pl.pallas_call(
        kernel,
        out_shape=(
            pltpu.VMEM((steps, channels, LANES), F32),
            pltpu.VMEM((channels, KINDS * LANES), F32),
        ),
        in_specs=[smem, smem, pl.BlockSpec(memory_space=pltpu.HBM), vmem],
        out_specs=(vmem, vmem),
        scratch_shapes=[
            pltpu.VMEM((len(TAPS), rows, columns), F32),
            pltpu.VMEM(frames.shape, frames.dtype),
            pltpu.SemaphoreType.DMA((channels // unroll,)),
        ],
        compiler_params=SMALL,
        name="frame_sums",
    )(
        taps, flags, pltpu.with_memory_space_constraint(frames, pltpu.HBM), *on_chip(pooling)
    )


def selection(rows):
    near = np.zeros((KINDS, LANES, len(TAPS), len(TAPS)), np.float32)
    edge = np.zeros((EDGE_KINDS, LANES, len(TAPS), len(TAPS)), np.float32)
    halo = np.zeros((2, HALO_KINDS, len(TAPS), len(TAPS)), np.float32)
    own = np.arange(rows)
    top, bottom = own[:DILATION_STEP], own[rows - DILATION_STEP :]
    for i, (a, b) in enumerate(TAPS):
        for j, (c, d) in enumerate(TAPS):
            down, across = c - a, d - b
            if (down, across) < (0, 0):
                down, across = -down, -across
            lag = abs(across)
            kind = down if across >= 0 else down + 2
            near[kind, lag * rows + own, i, j] += 1
            if down:
                halo[down - 1, across + 2, i, j] += 1
            for side, group in ((1, 0), (-1, 1)):
                if b == d == side:
                    near[5 + down, group * rows + own, i, j] -= 1
                    if down:
                        halo[down - 1, 5 + group, i, j] -= 1
            if a == c != 0:
                lost = top if a == 1 else bottom
                edge[0, lag * rows + lost, i, j] -= 1
                for side, group in ((1, 0), (-1, 1)):
                    if b == d == side:
                        edge[1, group * rows + lost, i, j] += 1
    pairs = len(TAPS) ** 2
    table = np.concatenate([m.reshape(-1, pairs) for m in (near, edge)], axis=0)
    halo = np.pad(halo.reshape(-1, pairs), ((0, -2 * HALO_KINDS % GROUP), (0, 0)))
    return [np.pad(m, ((0, 0), (0, LANES - pairs))) for m in (table, halo)]


def beside_tile():
    place, count = lax.axis_index("space"), lax.axis_size("space")
    has_above = jnp.where(place > 0, 1.0, 0.0).astype(F32)
    has_below = jnp.where(place < count - 1, 1.0, 0.0).astype(F32)
    return has_above, has_below


def spread():
    shape = (len(TAPS), LANES)
    source = lax.broadcasted_iota(jnp.int32, shape, 1)
    return source, lax.broadcasted_iota(jnp.int32, shape, 0)


def gain_kernel(flags, above, below, part, taps, pooling, gain, gain_part):
    steps, _, channels, columns = above.shape
    rows = pooling.shape[0]
    has_above, has_below = beside_tile()
    source, tap = spread()
    tap_columns = exact(taps[...], (source == tap).astype(F32), TN)
    halo_weights = []
    for a, start, has in ((-1, 0, has_above), (1, rows - DILATION_STEP, has_below)):
        for r in range(DILATION_STEP):
            value = jnp.zeros((channels, columns), F32)
            for b in (-1, 0, 1):
                k = TAPS.index((a, b))
                shifted = moved(pooling[start + r : start + r + 1, :], -DILATION_STEP * b, 1)
                value = value + tap_columns[:, k : k + 1] * shifted
            halo_weights.append(value * has)
    row_sums = []
    for t in range(steps):
        total = jnp.zeros((channels, columns), F32)
        for r in range(DILATION_STEP):
            total = total + above[t, r].astype(F32) * halo_weights[r]
            total = total + below[t, r].astype(F32) * halo_weights[DILATION_STEP + r]
        row_sums.append(part[t] + folded(total))
    ones = jnp.ones((GROUP, LANES), BF16)
    high, low = split(jnp.concatenate(row_sums, axis=0))
    tile_sums = contract(ones, high, NT) + contract(ones, low, NT)
    shape = (GROUP, steps * channels)
    owner = lax.broadcasted_iota(jnp.int32, shape, 1) // channels
    step = lax.broadcasted_iota(jnp.int32, shape, 0)
    seen = jnp.zeros(shape, F32)
    for t in range(steps):
        seen = jnp.where((owner == t) & (step == t), flags[t].astype(F32), seen)
    gains = jnp.concatenate([gain[...]] * steps, axis=0)
    product = three_pass(split(tile_sums * seen), split(gains), NN)
    gain_part[...] = product[:steps]


def gain_sums(flags, above, below, part, taps, pooling, gain):
    vmem = pl.BlockSpec(memory_space=pltpu.VMEM)
    smem = pl.BlockSpec(memory_space=pltpu.SMEM)
    return pl.pallas_call(
        gain_kernel,
        out_shape=jax.ShapeDtypeStruct((above.shape[0], gain.shape[1]), F32),
        in_specs=[smem] + [vmem] * 6,
        out_specs=vmem,
        compiler_params=SMALL,
        name="gain_sums",
    )(flags, *on_chip(above, below, part, taps, pooling, gain))


def gradient_kernel(
    scale, rows, flags, tops, bottoms, above, below, stats, taps, table, halo_table,
    gradient, values,
):
    steps, _, channels, columns = tops.shape
    has_above, has_below = beside_tile()
    sums = [[None] * 5 for _ in range(2)]
    for t in range(steps):
        flag = flags[t].astype(F32)
        for r in range(DILATION_STEP):
            near_top = tops[t, DILATION_STEP + r].astype(F32)
            far_bottom = bottoms[t, r].astype(F32)
            near_bottom = bottoms[t, DILATION_STEP + r].astype(F32)
            high = above[t, r].astype(F32) * (flag * has_above)
            low = below[t, r].astype(F32) * (flag * has_below)
            for n in range(-2, 3):
                shifted_low = moved(low, DILATION_STEP * n, 1)
                shifted_high = moved(high, -DILATION_STEP * n, 1)
                one = near_bottom * shifted_low
                two = far_bottom * shifted_low + near_top * shifted_high
                for which, value in ((0, one), (1, two)):
                    old = sums[which][n]
                    sums[which][n] = value if old is None else old + value
    values[:, : KINDS * LANES] = stats[...]
    lane = lax.rem(lax.broadcasted_iota(jnp.int32, (channels, LANES), 1), rows)
    outside = jnp.where(lane < DILATION_STEP, 1.0 - has_above, 0.0)
    outside = jnp.where(lane >= rows - DILATION_STEP, 1.0 - has_below, outside)
    at = KINDS * LANES
    for kind in (0, 5):
        values[:, at : at + LANES] = stats[:, kind * LANES : (kind + 1) * LANES] * outside
        at += LANES
    high, low = split(values[...])
    pairs = contract(high, table[...], NN) + contract(low, table[...], NN)
    lane = lax.broadcasted_iota(jnp.int32, (channels, LANES), 1)
    for which in range(2):
        pieces = [folded(sums[which][n]) for n in range(-2, 3)]
        centre = sums[which][0]
        pieces.append(jnp.where(lane < DILATION_STEP, centre[:, :LANES], 0.0))
        pieces.append(
            jnp.where(lane >= LANES - DILATION_STEP, centre[:, columns - LANES :], 0.0)
        )
        for n, piece in enumerate(pieces):
            at = which * HALO_KINDS + n
            pairs = pairs + jnp.sum(piece, axis=1, keepdims=True) * halo_table[at : at + 1, :]
    source, tap = spread()
    weights = exact(taps[...], (source // len(TAPS) == tap).astype(F32), TN)
    gathered = (source % len(TAPS) == tap).astype(F32)
    gradient[...] = exact(gathered, pairs * weights, NT) * scale


def tap_sums(flags, tops, bottoms, above, below, stats, taps, rows):
    _, _, channels, columns = tops.shape
    scale = 1.0 / (rows * lax.axis_size("space") * columns)
    table, halo_table = selection(rows)
    table = jnp.asarray(table, BF16)
    vmem = pl.BlockSpec(memory_space=pltpu.VMEM)
    smem = pl.BlockSpec(memory_space=pltpu.SMEM)

    def kernel(*refs):
        gradient_kernel(scale, rows, *refs)

    return pl.pallas_call(
        kernel,
        out_shape=jax.ShapeDtypeStruct((len(TAPS), channels), F32),
        in_specs=[smem] + [vmem] * 8,
        out_specs=vmem,
        scratch_shapes=[pltpu.VMEM((channels, table.shape[0]), F32)],
        compiler_params=SMALL,
        name="tap_sums",
    )(flags, *on_chip(tops, bottoms, above, below, stats, taps, table, jnp.asarray(halo_table)))


def beside(top, bottom, axis):
    count = lax.axis_size(axis)
    if count == 2:
        sent = jnp.where(lax.axis_index(axis) == 0, bottom, top)
        got = lax.ppermute(sent, axis, [(0, 1), (1, 0)])
        return got, got
    forward = [(i, (i + 1) % count) for i in range(count)]
    backward = [(target, source) for source, target in forward]
    return lax.ppermute(bottom, axis, forward), lax.ppermute(top, axis, backward)


def partner(value, axis):
    if lax.axis_size(axis) == 2:
        return lax.ppermute(value, axis, [(0, 1), (1, 0)])
    return lax.psum(value, axis) - value


def total(value, axis):
    if lax.axis_size(axis) == 2:
        return added(value, partner(value, axis))
    return lax.psum(value, axis)


def local(
    frames,
    conv_taps,
    pooling,
    gain_matrix,
    transition,
    update_map,
    quiet_root,
    observed_root,
    init_mean,
    init_root,
    observed,
):
    step_count, channels, rows, _ = frames.shape
    place = lax.axis_index("tm").astype(jnp.int32)[None]
    flags = history(observed[None], "tm")
    tops = frames[:, :, :EDGE].transpose(0, 2, 1, 3)
    bottoms = frames[:, :, rows - EDGE :].transpose(0, 2, 1, 3)
    above, below = beside(tops[:, :DILATION_STEP], bottoms[:, DILATION_STEP:], "space")
    taps, gain = conv_taps.T, gain_matrix.T
    span = 2 if step_count % 2 == 0 else 1
    part, stats = frame_sums(taps, observed, frames, pooling)
    gain_part = gain_sums(observed, above, below, part, taps, pooling, gain)
    gradient = tap_sums(observed, tops, bottoms, above, below, stats, taps, rows)
    map_high, map_low, span_high, span_low, span_gram, first_gram = prepare(
        span, transition, update_map, quiet_root, observed_root, init_root
    )
    if lax.axis_size("chan") == 2 and step_count <= TAP_ROW:
        both = packed(gain_part, partner(gain_part, "chan"), gradient)
        both_beside = partner(both, "space")
        shifts = first_sum(both, both_beside, step_count)
    else:
        both = jnp.pad(
            gradient,
            ((TAP_ROW, 2 * GROUP - len(TAPS)), (0, gain.shape[1] - channels)),
        )
        shifts = total(total(gain_part, "chan"), "space")[None]
        both_beside = partner(both, "space")
    held = history(shifts, "tm")
    gram = recursion(place, flags, step_count, span, span_high, span_low, span_gram, first_gram)
    tops = factor_top(gram)
    root, filtered_means, gradient = factor(
        place, flags, step_count, span, gram, tops,
        map_high, map_low, span_high, span_low, held, init_mean, both, both_beside, channels,
    )
    return (filtered_means, root[None], gradient.transpose(1, 2, 0))


def solution(mesh):
    return jax.shard_map(
        local,
        mesh=mesh,
        in_specs=(
            P(("groups", "tm"), "chan", "space", None),
            P("chan", None),
            P("space", None),
            P(None, ("space", "chan")),
            P(),
            P(),
            P(),
            P(),
            P("groups"),
            P("groups", None),
            P(("groups", "tm")),
        ),
        out_specs=(
            P(("groups", "tm"), None),
            P(("groups", "tm"), None, None),
            P(("groups", "tm"), "chan", None),
        ),
        check_vma=False,
    )
```
